32 devices in a mesh: region: 4 (over x, core), sector: 8 (over z, y).
Axes of the slice: x: 2, y: 2, z: 4, core: 2. Of those that a mesh axis runs over, the one named last changes fastest.
Arguments:
- start_state: bfloat16 [4, 32, 128, 4, 128], P('region', 'sector'), may hold values from -6 to 6
- left_env: bfloat16 [4, 32, 16, 128, 128], P('region', 'sector'), may hold values from -0.125 to 0.125
- right_env: bfloat16 [4, 32, 16, 128, 128], P('region', 'sector'), may hold values from -0.5 to 0.5
- mpo_tensor: bfloat16 [16, 4, 4, 16], replicated, may hold values from -0.75 to 0.75
- decay: float32 [4, 32, 128], P('region', 'sector'), may hold values from 0.15 to 1
- energy_terms: float32 [4, 32, 128], P('region', 'sector'), may hold values from -1.2 to 1.2
- live_count: int32 [4, 8], P('region', 'sector'), may hold values from 1 to 4, as said below
Outputs:
- state_out: bfloat16 [4, 32, 128, 4, 128], P('region', 'sector')
- density: float32 [4, 32, 128, 128], P('region', 'sector')
- energy: float32 [4], P('region')
The draws below stay inside these ranges and needn't reach their ends.
Inputs may be any that keep to these rules, and one draw needn't show every extreme that they name: `live_count`: each device's live blocks fill its first slots; some device holds 4 live blocks.
All inputs are finite; a program needn't handle non-finite values.
Results may differ from the reference program's by a relative error of at most 0.0055.
The reference program's roundings to bfloat16 on the way (of `contract_right` and `contract_mpo`) count: a program that leaves them out, or rounds other values in their place, can miss the bound.
Values may be sent and summed in bfloat16 or wider, within the bound.
A program may use at most 64 MiB of HBM per device.

```python
import math
import jax
import jax.numpy as jnp
from jax import lax

BLK = 128
PHYS = 4
CHAN = 16
SLOTS = 4
DAV = 2
LATTICE_PARTS = 4
SECTORS = 8
BLOCKS = 32


def draw_decay(key, part):
    stochastic_seeds = jax.random.split(key, 5)
    array_dimensions = (LATTICE_PARTS, BLOCKS, BLK)
    slow_share = 0.5
    channel_pick = jax.random.uniform(stochastic_seeds[0], (1, BLOCKS, BLK), jnp.float32)
    is_slow = channel_pick < slow_share
    rate_draw = jax.random.uniform(stochastic_seeds[1], (1, BLOCKS, BLK), jnp.float32, 0.2, 1.2)
    tardy_lines = jnp.exp(-rate_draw / LATTICE_PARTS) * jnp.ones(array_dimensions, jnp.float32)
    fast_rows = jax.random.uniform(stochastic_seeds[2], array_dimensions, jnp.float32, 0.3, 0.7)
    spurt_extent = jax.random.uniform(stochastic_seeds[3], array_dimensions, jnp.float32) < 1.5 / LATTICE_PARTS
    spurt_ceiling = jax.random.uniform(stochastic_seeds[4], array_dimensions, jnp.float32, 0.5, 0.8)
    tardy_lines = jnp.where(spurt_extent, tardy_lines * spurt_ceiling, tardy_lines)
    return jnp.where(is_slow, tardy_lines, fast_rows).astype(jnp.float32)


def draw_live_count(key, part):
    stochastic_seeds = jax.random.split(key, 3)
    first_draw = jax.random.randint(stochastic_seeds[0], (LATTICE_PARTS, SECTORS), 0, SLOTS)
    second_draw = jax.random.randint(stochastic_seeds[1], (LATTICE_PARTS, SECTORS), 0, SLOTS)
    counts = 1 + first_draw * second_draw // max(SLOTS - 1, 1)
    chosen = jax.random.randint(stochastic_seeds[2], (), 0, LATTICE_PARTS * SECTORS)
    flat_counts = jnp.where(jnp.arange(LATTICE_PARTS * SECTORS, dtype=jnp.int32) == chosen, SLOTS, counts.reshape(-1))
    return flat_counts.reshape(LATTICE_PARTS, SECTORS).astype(jnp.int32)


def steps_of(rng, extent, cuts, low, largest):
    def one(position, blocks):
        steps = jax.random.uniform(jax.random.fold_in(jax.random.fold_in(rng, 6), position), (blocks,), jnp.float32, low / len(cuts), largest / len(cuts))
        return jnp.repeat(jnp.exp(steps), extent[position] // blocks).reshape((-1,) + (1,) * (len(extent) - position - 1))

    factor_of = one(*cuts[0])
    for cut in cuts[1:]:
        factor_of = factor_of * one(*cut)
    return factor_of


def bell_draw(rng, shape, width, limit, shards=(), kind=jnp.bfloat16):
    array = width * jax.random.normal(rng, shape, jnp.float32)
    if shards:
        array = array * steps_of(rng, shape, shards, -0.22, 0.18)
    return jnp.clip(array, -limit, limit).astype(kind)


def setup_inputs(seed: int = 0) -> dict:
    key_list = jax.random.split(jax.random.key(seed), 8)
    return {
        "start_state": bell_draw(key_list[0], (LATTICE_PARTS, BLOCKS, BLK, PHYS, BLK), 1.0, 6.0, ((0, 4), (1, 8))),
        "left_env": bell_draw(key_list[1], (LATTICE_PARTS, BLOCKS, CHAN, BLK, BLK), (CHAN * BLK) ** -0.5, 0.125, ((0, 4), (1, 8))),
        "right_env": bell_draw(key_list[2], (LATTICE_PARTS, BLOCKS, CHAN, BLK, BLK), BLK ** -0.5, 0.5, ((0, 4), (1, 8))),
        "mpo_tensor": bell_draw(key_list[3], (CHAN, PHYS, PHYS, CHAN), (PHYS * CHAN) ** -0.5, 0.75),
        "decay": draw_decay(jax.random.fold_in(key_list[7], 71), 0),
        "energy_terms": bell_draw(key_list[5], (LATTICE_PARTS, BLOCKS, BLK), 0.2, 1.2, ((0, 4), (1, 8)), jnp.float32),
        "live_count": draw_live_count(jax.random.fold_in(key_list[7], 71), 0),
    }


epsilon = 1e-06

def apply_block(vector, left_part, right_part, mpo_tensor, offset):
    vector_wide = vector.astype(jnp.float32)
    contract_right = jnp.einsum('asc,wcb->aswb', vector_wide, right_part.astype(jnp.float32)).astype(jnp.bfloat16)
    contract_mpo = jnp.einsum('vstw,atwb->asvb', mpo_tensor.astype(jnp.float32), contract_right.astype(jnp.float32)).astype(jnp.bfloat16)
    applied = jnp.einsum('vac,csvb->asb', left_part.astype(jnp.float32), contract_mpo.astype(jnp.float32))
    return applied + offset[:, None, None] * vector_wide

def accumulate(running, row_pair):
    return (row_pair[0] * running + row_pair[1], running)

def reference(start_state, left_env, right_env, mpo_tensor, decay, energy_terms, live_count):
    initial = jnp.zeros((BLOCKS, BLK), jnp.float32)
    unused, offsets = lax.scan(accumulate, initial, (decay, energy_terms))
    scale = math.sqrt(BLOCKS * BLK * PHYS * BLK)

    def region_solve(region_index):
        previous = jnp.maximum(region_index - 1, 0).astype(jnp.int32)
        left_part = lax.dynamic_index_in_dim(left_env, previous, 0, keepdims=False)
        right_part = lax.dynamic_index_in_dim(right_env, region_index, 0, keepdims=False)
        starting = lax.dynamic_index_in_dim(start_state, region_index, 0, keepdims=False)
        offset_rows = lax.dynamic_index_in_dim(offsets, region_index, 0, keepdims=False)
        counts = lax.dynamic_index_in_dim(live_count, region_index, 0, keepdims=False)
        slot_ids = jnp.arange(BLOCKS, dtype=jnp.int32)
        live_mask = slot_ids % SLOTS < counts[slot_ids // SLOTS]

        def operate(vector_bf):

            def count_per_block(block_items):
                vector, left_one, right_one, offset_one, is_active_region = block_items
                return lax.cond(is_active_region, lambda operands: apply_block(operands[0], operands[1], operands[2], mpo_tensor, operands[3]), lambda operands: jnp.zeros(operands[0].shape, jnp.float32), (vector, left_one, right_one, offset_one))
            return lax.map(count_per_block, (vector_bf, left_part, right_part, offset_rows, live_mask))
        first = starting.astype(jnp.float32) * live_mask.astype(jnp.float32)[:, None, None, None]
        norm_sum = jnp.sum(first * first)
        inverse = lax.rsqrt(norm_sum + epsilon)
        current = first * inverse
        applied = operate(first.astype(jnp.bfloat16)) * inverse
        for iteration in range(DAV):
            quotient = jnp.sum(current * applied)
            residual = applied - quotient * current
            resid_sq = jnp.sum(residual * residual)
            factor = lax.rsqrt(resid_sq + epsilon)
            search = residual * factor
            probe_mapped_vector = operate(search.astype(jnp.bfloat16))
            curvature = jnp.sum(search * probe_mapped_vector)
            rotation = 0.5 * jnp.arctan2(-2.0 * resid_sq * factor, curvature - quotient)
            cos_part = jnp.cos(rotation)
            sin_part = jnp.sin(rotation)
            current = cos_part * current + sin_part * search
            applied = cos_part * applied + sin_part * probe_mapped_vector
        energy = jnp.sum(current * applied)
        state_out = (scale * current).astype(jnp.bfloat16)
        state_wide = state_out.astype(jnp.float32)
        density = jnp.einsum('nasb,ncsb->nac', state_wide, state_wide) / (PHYS * BLK)
        return (state_out, density, energy)
    state_out, density, energy = lax.map(region_solve, jnp.arange(LATTICE_PARTS, dtype=jnp.int32))
    return (state_out, density, energy)
```

```python
import functools
import math

import jax
import jax.numpy as jnp
from jax import lax
from jax.experimental import pallas as pl
from jax.experimental.pallas import tpu as pltpu
from jax.sharding import PartitionSpec as P

DAV = 2
EPS = 1e-06
MESH = pl.DeviceIdType.MESH
F32 = jnp.float32
BF16 = jnp.bfloat16
PAD = 8


def half_rotation(y, x):
    top = jnp.maximum(jnp.abs(x), jnp.abs(y))
    safe = jnp.where(top > 0, top, 1.0)
    xn, yn = x / safe, y / safe
    h = jnp.sqrt(xn * xn + yn * yn)
    h = jnp.where(top > 0, h, 1.0)
    big = jnp.sqrt(0.5 * (h + jnp.abs(xn)) / h)
    small = jnp.abs(yn) / (2.0 * h * big)
    big = jnp.where(top > 0, big, 1.0)
    small = jnp.where(top > 0, small, 0.0)
    cos_part = jnp.where(x >= 0, big, small)
    sin_size = jnp.where(x >= 0, small, big)
    return cos_part, jnp.where(y > 0, sin_size, -sin_size)


def kernel(
    regions, sectors, start, left, right, operator, decay, energy, live,
    state_out, energy_out,
    start_in, left_in, left_t, right_in, right_t, planes, rows_buf, mixed, lines, spread,
    base0, base1, base2, image, decay_all, energy_all, shift, part, gathered,
    left_send, left_recv, right_sem, own_sem, start_sem, pre_send, pre_recv, sum_send, sum_recv,
):
    slots, chan, blk, _ = left.shape
    phys = start.shape[1] // blk
    wide = phys * blk
    me, mine = lax.axis_index("region"), lax.axis_index("sector")
    group = 256 // (phys * chan)
    pair = 2 * group
    for n in range(slots):
        pltpu.make_async_copy(right.at[n], right_in.at[n], right_sem.at[n]).start()
        pltpu.make_async_copy(start.at[n], start_in.at[n], start_sem.at[n]).start()

    barrier = pltpu.get_barrier_semaphore()
    for k in range(1, regions):
        pl.semaphore_signal(
            barrier, 1, device_id={"region": lax.rem(me + k, regions)}, device_id_type=MESH
        )
    for k in range(1, sectors):
        pl.semaphore_signal(
            barrier, 1, device_id={"sector": lax.rem(mine + k, sectors)}, device_id_type=MESH
        )
    pl.semaphore_wait(barrier, regions + sectors - 2)

    def left_copy(n):
        return pltpu.make_async_remote_copy(
            src_ref=left.at[n], dst_ref=left_in.at[n],
            send_sem=left_send.at[n], recv_sem=left_recv.at[n],
            device_id={"region": lax.rem(me + 1, regions)}, device_id_type=MESH,
        )

    def own_copy(n):
        return pltpu.make_async_copy(left.at[n], left_in.at[n], own_sem.at[n])

    def prefix_copies(k, slot):
        to = {"region": lax.rem(me + k, regions)}
        return [
            pltpu.make_async_remote_copy(
                src_ref=src, dst_ref=dst.at[slot],
                send_sem=pre_send.at[i, k - 1], recv_sem=pre_recv.at[i, k - 1],
                device_id=to, device_id_type=MESH,
            )
            for i, (src, dst) in enumerate(((decay, decay_all), (energy, energy_all)))
        ]

    for k in range(1, regions):
        for copy in prefix_copies(k, me):
            copy.start()

    @pl.when(me < regions - 1)
    def _():
        for n in range(slots):
            left_copy(n).start()

    @pl.when(me == 0)
    def _():
        for n in range(slots):
            own_copy(n).start()

    decay_all[me] = decay[...]
    energy_all[me] = energy[...]
    for k in range(1, regions):
        for copy in prefix_copies(k, lax.rem(me + regions - k, regions)):
            copy.wait()
    offsets = jnp.zeros((slots, blk), F32)
    for p in range(regions - 1):
        offsets = jnp.where(p < me, decay_all[p] * offsets + energy_all[p], offsets)
    shift[...] = offsets

    live_slots = live[...]

    side = group * phys * chan
    lines[...] = operator[...].astype(F32)

    def where_one(test):
        return jnp.where(test, 1.0, 0.0).astype(BF16)

    def grid_of(shape):
        return [lax.broadcasted_iota(jnp.int32, shape, i) for i in range(2)]

    r, c = grid_of((side, chan * phys))
    pick_row = where_one((r // (group * phys) == c // phys) & (r % phys == c % phys))
    r, c = grid_of((chan, side))
    total = jnp.zeros((side, side), F32)
    for t in range(phys):
        tall = jnp.dot(
            pick_row,
            lines[pl.ds(t, chan * phys, stride=phys), :].astype(BF16),
            preferred_element_type=F32,
        ).astype(BF16)
        pick_column = where_one((c // (group * chan) == t) & (c % chan == r))
        total = total + jnp.dot(tall, pick_column, preferred_element_type=F32)
    r, c = grid_of((side, side))
    same = (r // phys) % group == (c // chan) % group
    spread[...] = jnp.where(same, total, 0.0).astype(BF16)

    def prepare_right(n):
        pltpu.make_async_copy(right.at[n], right_in.at[n], right_sem.at[n]).wait()
        pitch = blk + PAD
        for w in range(chan):
            planes[w * pitch : w * pitch + blk, :] = right_in[n, w].astype(F32).T
        for b in range(blk):
            right_t[n, b * chan : (b + 1) * chan, :] = planes[
                pl.ds(b, chan, stride=pitch), :
            ].astype(BF16)

    def prepare_left(n):
        for u in range(chan):
            left_t[n, u * blk : (u + 1) * blk, :] = left_in[n, u].T

    def sum8(value):
        return jnp.sum(value.reshape(-1, 8, value.shape[-1]), axis=0)

    def operate(n, slot, vector, arrive):
        half = group * chan
        for j in range(blk // pair):
            rows = right_t[n, j * pair * chan : (j + 1) * pair * chan, :]
            first = jnp.dot(rows, vector, preferred_element_type=F32).astype(BF16)
            stacked = [
                jnp.concatenate(
                    [
                        first[g * half : (g + 1) * half, t * blk : (t + 1) * blk]
                        for t in range(phys)
                    ],
                    axis=0,
                )
                for g in range(2)
            ]
            second = jnp.dot(
                spread[...], jnp.concatenate(stacked, axis=1), preferred_element_type=F32
            ).astype(BF16)
            tile = group * phys
            for g in range(2):
                row = (2 * j + g) * tile
                for u in range(chan):
                    mixed[slot, row : row + tile, u * blk : (u + 1) * blk] = second[
                        u * tile : (u + 1) * tile, g * blk : (g + 1) * blk
                    ]
        arrive()
        rows_buf[slot] = jnp.dot(mixed[slot], left_t[n], preferred_element_type=F32)
        return [rows_buf[slot, pl.ds(s, blk, stride=phys), :] for s in range(phys)]

    def spread_sum(total):
        return jnp.broadcast_to(jnp.sum(total, keepdims=True).reshape(1, 1), (1, blk))

    def length_of(square, whole):
        square = jnp.maximum(square, 1e-10 * whole)
        inverse = jnp.where(square > 0, lax.rsqrt(jnp.where(square > 0, square, 1.0)), 0.0)
        return square * inverse, inverse

    def share_of(value, norm):
        return jnp.where(norm > 0, value / jnp.where(norm > 0, norm, 1.0), 0.0)

    zero = jnp.zeros((8, blk), F32)
    lane = lax.broadcasted_iota(jnp.int32, (1, blk), 1)

    def solve_slot(n, carry):
        prepare_right(n)
        alive = jnp.broadcast_to(jnp.where(n < live_slots, 1.0, 0.0), (1, blk)).astype(F32)
        pltpu.make_async_copy(start.at[n], start_in.at[n], start_sem.at[n]).wait()
        rows_buf[0] = start_in[n].astype(F32)
        firsts = []
        for t in range(phys):
            first = rows_buf[0, pl.ds(t, blk, stride=phys), :].T * alive
            base0[n, t] = first
            firsts.append(first.astype(BF16))
        offset = shift[pl.ds(n, 1)]

        def arrive():
            @pl.when(me > 0)
            def _():
                left_copy(n).wait_recv()

            @pl.when(me == 0)
            def _():
                own_copy(n).wait()

            prepare_left(n)

        results = operate(n, 0, jnp.concatenate(firsts, axis=1), arrive)
        ff, fa, aa = zero, zero, zero
        for s in range(phys):
            first = base0[n, s]
            value = results[s] + offset * first
            image[s] = value
            ff, fa, aa = ff + sum8(first * first), fa + sum8(first * value), aa + sum8(value * value)
        ff, fa, aa = spread_sum(ff), spread_sum(fa), spread_sum(aa)
        sigma = share_of(fa, ff)
        rho1, inverse = length_of(aa - sigma * fa, aa)

        probes = []
        g01, g11 = zero, zero
        for t in range(phys):
            first = base0[n, t]
            probe = (image[t] - sigma * first) * inverse
            base1[n, t] = probe
            g01, g11 = g01 + sum8(first * probe), g11 + sum8(probe * probe)
            probes.append(probe.astype(BF16))
        results = operate(n, 0, jnp.concatenate(probes, axis=1), lambda: None)
        fa, pa, aa = zero, zero, zero
        for s in range(phys):
            probe = base1[n, s]
            value = results[s] + offset * probe.astype(BF16).astype(F32)
            image[s] = value
            fa, pa, aa = fa + sum8(base0[n, s] * value), pa + sum8(probe * value), aa + sum8(value * value)
        g01, g11, fa, pa, aa = spread_sum(g01), spread_sum(g11), spread_sum(fa), spread_sum(pa), spread_sum(aa)
        alpha, beta = share_of(fa, ff), share_of(pa, g11)
        rho2, inverse = length_of(aa - alpha * fa - beta * pa, aa)

        probes = []
        g02, g12, g22 = zero, zero, zero
        for t in range(phys):
            probe = (image[t] - alpha * base0[n, t] - beta * base1[n, t]) * inverse
            base2[n, t] = probe
            g02, g12, g22 = g02 + sum8(base0[n, t] * probe), g12 + sum8(base1[n, t] * probe), g22 + sum8(probe * probe)
            probes.append(probe.astype(BF16))
        results = operate(n, 0, jnp.concatenate(probes, axis=1), lambda: None)
        g03, g13, g23 = zero, zero, zero
        for s in range(phys):
            probe = base2[n, s]
            value = results[s] + offset * probe.astype(BF16).astype(F32)
            g03, g13, g23 = g03 + sum8(base0[n, s] * value), g13 + sum8(base1[n, s] * value), g23 + sum8(probe * value)
        numbers = [ff, sigma, rho1, g01, g11, alpha, beta, rho2]
        numbers += [spread_sum(g) for g in (g02, g12, g22, g03, g13, g23)]
        here = lane == mine * slots + n
        for i, number in enumerate(numbers):
            part[i : i + 1] = jnp.where(here, number, part[i : i + 1])
        return carry

    part[...] = jnp.zeros_like(part)
    lax.fori_loop(0, slots, solve_slot, 0)

    gathered[mine] = part[...]

    def copy_of(k, slot):
        return pltpu.make_async_remote_copy(
            src_ref=part, dst_ref=gathered.at[slot],
            send_sem=sum_send.at[k - 1], recv_sem=sum_recv.at[k - 1],
            device_id={"sector": lax.rem(mine + k, sectors)}, device_id_type=MESH,
        )

    for k in range(1, sectors):
        copy_of(k, mine).start()
    for k in range(1, sectors):
        copy_of(k, lax.rem(mine + sectors - k, sectors)).wait()
    table = gathered[0]
    for i in range(1, sectors):
        table = table + gathered[i]
    (
        g00, sigma, rho1, g01, g11, alpha, beta, rho2, g02, g12, g22, g03, g13, g23,
    ) = [table[i : i + 1] for i in range(14)]
    gram = {
        (0, 0): g00, (0, 1): g01, (0, 2): g02, (0, 3): g03, (1, 1): g11, (1, 2): g12, (1, 3): g13,
        (2, 2): g22, (2, 3): g23,
    }

    def inner(x, y):
        total = jnp.zeros((1, blk), F32)
        for i, xi in enumerate(x):
            for j, yj in enumerate(y):
                if xi is not None and yj is not None:
                    total = total + xi * yj * gram[min(i, j), max(i, j)]
        return jnp.broadcast_to(jnp.sum(total, axis=1, keepdims=True), (1, blk))

    def mix(p, x, q, y):
        def one(a, b):
            if a is None:
                return None if b is None else q * b
            return p * a if b is None else p * a + q * b

        return [one(a, b) for a, b in zip(x, y)]

    images = [[sigma, rho1, None, None], [alpha, beta, rho2, None], [None, None, None, jnp.ones((1, blk), F32)]]
    unit = jnp.ones((1, blk), F32)
    inverse = lax.rsqrt(inner([unit], [unit]) + EPS)
    current = [inverse * unit, None, None, None]
    applied = [inverse * a if a is not None else None for a in images[0]]
    for turn in range(DAV):
        quotient = inner(current, applied)
        residual = mix(1.0, applied, -quotient, current)
        resid_sq = inner(residual, residual)
        factor = lax.rsqrt(resid_sq + EPS)
        search = [factor * a if a is not None else None for a in residual]
        moved = [None] * 4
        for a, line in zip(search, images):
            if a is not None:
                moved = mix(1.0, moved, a, line)
        curvature = inner(search, moved)
        cos_part, sin_part = half_rotation(-2.0 * resid_sq * factor, curvature - quotient)
        current = mix(cos_part, current, sin_part, search)
        applied = mix(cos_part, applied, sin_part, moved)
    energy_out[...] = jnp.broadcast_to(inner(current, applied), (8, blk))
    scale = math.sqrt(slots * sectors * blk * phys * blk)

    for n in range(slots):
        here = lane == mine * slots + n
        c0, c1, c2 = [
            jnp.broadcast_to(jnp.sum(jnp.where(here, scale * c, 0.0), axis=1, keepdims=True), (1, blk))
            for c in current[:3]
        ]
        for t in range(phys):
            state = c0 * base0[n, t] + c1 * base1[n, t] + c2 * base2[n, t]
            state_out[n, t] = state.astype(BF16)

    @pl.when(me < regions - 1)
    def _():
        for n in range(slots):
            left_copy(n).wait_send()


def finish(state, energy, out, density, energy_out, rows_buf, out_buf, density_buf, sems):
    slots, phys, blk, _ = state.shape
    copies = []
    for n in range(slots):
        total = jnp.zeros((blk, blk), F32)
        for s in range(phys):
            turned = state[n, s].T
            rows_buf[n, pl.ds(s, blk, stride=phys), :] = turned.astype(F32)
            total = total + jnp.dot(turned, state[n, s], preferred_element_type=F32)
        out_buf[n] = rows_buf[n].astype(BF16)
        density_buf[n] = total / (phys * blk)
        for i, (src, dst) in enumerate(((out_buf, out), (density_buf, density))):
            copies.append(pltpu.make_async_copy(src.at[n], dst.at[n], sems.at[i, n]))
            copies[-1].start()
    energy_out[0] = energy[0, 0]
    for copy in copies:
        copy.wait()


def body(regions, sectors, start_state, left_env, right_env, mpo_tensor, decay, energy_terms, live_count):
    _, slots, blk, phys, _ = start_state.shape
    chan = left_env.shape[2]
    wide = phys * blk
    group = 256 // (phys * chan)
    vmem = pl.BlockSpec(memory_space=pltpu.VMEM)
    hbm = pl.BlockSpec(memory_space=pl.ANY)
    smem = pl.BlockSpec(memory_space=pltpu.SMEM)
    dma = pltpu.SemaphoreType.DMA
    state = pltpu.VMEM((slots, phys, blk, blk), F32)
    outs = pl.pallas_call(
        functools.partial(kernel, regions, sectors),
        out_shape=(
            jax.ShapeDtypeStruct((slots, phys, blk, blk), BF16),
            jax.ShapeDtypeStruct((8, blk), F32),
        ),
        in_specs=[hbm, hbm, hbm, vmem, vmem, vmem, vmem],
        out_specs=(vmem, vmem),
        scratch_shapes=[
            pltpu.VMEM((slots, wide, blk), BF16),
            pltpu.VMEM((slots, chan, blk, blk), BF16),
            pltpu.VMEM((slots, chan * blk, blk), BF16),
            pltpu.VMEM((slots, chan, blk, blk), BF16),
            pltpu.VMEM((slots, chan * blk, blk), BF16),
            pltpu.VMEM((chan * (blk + PAD), blk), F32),
            pltpu.VMEM((2, wide, blk), F32),
            pltpu.VMEM((2, wide, chan * blk), BF16),
            pltpu.VMEM((chan * phys * phys, chan), F32),
            pltpu.VMEM((group * phys * chan, group * phys * chan), BF16),
            state, state, state, pltpu.VMEM((phys, blk, blk), F32),
            pltpu.VMEM((regions, slots, blk), F32),
            pltpu.VMEM((regions, slots, blk), F32),
            pltpu.VMEM((slots, blk), F32),
            pltpu.VMEM((16, blk), F32),
            pltpu.VMEM((sectors, 16, blk), F32),
            dma((slots,)), dma((slots,)), dma((slots,)), dma((slots,)), dma((slots,)),
            dma((2, regions)), dma((2, regions)),
            dma((sectors,)), dma((sectors,)),
        ],
        compiler_params=pltpu.CompilerParams(collective_id=0, has_side_effects=True),
    )(
        start_state.reshape(slots, wide, blk), left_env[0], right_env[0],
        mpo_tensor.reshape(chan * phys * phys, chan),
        decay[0], energy_terms[0], live_count,
    )
    state_out, density, energy = pl.pallas_call(
        finish,
        out_shape=(
            jax.ShapeDtypeStruct((slots, wide, blk), BF16),
            jax.ShapeDtypeStruct((slots, blk, blk), F32),
            jax.ShapeDtypeStruct((1,), F32),
        ),
        in_specs=[vmem, vmem],
        out_specs=(hbm, hbm, smem),
        scratch_shapes=[
            pltpu.VMEM((slots, wide, blk), F32),
            pltpu.VMEM((slots, wide, blk), BF16),
            pltpu.VMEM((slots, blk, blk), F32),
            dma((2, slots)),
        ],
    )(*outs)
    return (
        state_out.reshape(start_state.shape),
        density.reshape(1, slots, blk, blk),
        energy,
    )


def solution(mesh):
    in_specs = (
        P("region", "sector", None, None, None),
        P("region", "sector", None, None, None),
        P("region", "sector", None, None, None),
        P(),
        P("region", "sector", None),
        P("region", "sector", None),
        P("region", "sector"),
    )
    out_specs = (
        P("region", "sector", None, None, None),
        P("region", "sector", None, None),
        P("region"),
    )
    step = functools.partial(body, mesh.shape["region"], mesh.shape["sector"])
    return jax.shard_map(step, mesh=mesh, in_specs=in_specs, out_specs=out_specs, check_vma=False)
```

```python
import functools
import math

import jax
import jax.numpy as jnp
from jax import lax
from jax.experimental import pallas as pl
from jax.experimental.pallas import tpu as pltpu
from jax.sharding import PartitionSpec as P

DAV = 2
EPS = 1e-06
MESH = pl.DeviceIdType.MESH
F32 = jnp.float32
BF16 = jnp.bfloat16
STEPS = DAV + 1
TILE = 16


def half_rotation(y, x):
    top = jnp.maximum(jnp.abs(x), jnp.abs(y))
    safe = jnp.where(top > 0, top, 1.0)
    xn, yn = x / safe, y / safe
    h = jnp.sqrt(xn * xn + yn * yn)
    h = jnp.where(top > 0, h, 1.0)
    big = jnp.sqrt(0.5 * (h + jnp.abs(xn)) / h)
    small = jnp.abs(yn) / (2.0 * h * big)
    big = jnp.where(top > 0, big, 1.0)
    small = jnp.where(top > 0, small, 0.0)
    cos_part = jnp.where(x >= 0, big, small)
    sin_size = jnp.where(x >= 0, small, big)
    return cos_part, jnp.where(y > 0, sin_size, -sin_size)


def kernel(
    regions, sectors, start, left, right, operator, decay, energy, live,
    state_out, energy_out,
    start_in, left_in, right_in, lines, spread, flipped, column,
    vector_a, vector_b, inner_a, inner_b, mixed_a, mixed_b, value_a, value_b,
    basis_a, basis_b, norms_a, norms_b, decay_all, energy_all, part, gathered,
    left_send, left_recv, right_sem, start_sem, pre_send, pre_recv, sum_send, sum_recv,
):
    slots, chan, blk, _ = left.shape
    wide = start.shape[1]
    phys = wide // blk
    me, mine = lax.axis_index("region"), lax.axis_index("sector")
    group = TILE // phys
    side = chan * TILE
    pairs = slots // 2
    rounds = pairs * STEPS
    for n in range(slots):
        pltpu.make_async_copy(right.at[n], right_in.at[n], right_sem.at[n]).start()
        pltpu.make_async_copy(start.at[n], start_in.at[n], start_sem.at[n]).start()

    barrier = pltpu.get_barrier_semaphore()
    for k in range(1, regions):
        pl.semaphore_signal(
            barrier, 1, device_id={"region": lax.rem(me + k, regions)}, device_id_type=MESH
        )
    for k in range(1, sectors):
        pl.semaphore_signal(
            barrier, 1, device_id={"sector": lax.rem(mine + k, sectors)}, device_id_type=MESH
        )
    pl.semaphore_wait(barrier, regions + sectors - 2)

    def left_copy(n):
        return pltpu.make_async_remote_copy(
            src_ref=left.at[n], dst_ref=left_in.at[n],
            send_sem=left_send.at[n], recv_sem=left_recv.at[n],
            device_id={"region": lax.rem(me + 1, regions)}, device_id_type=MESH,
        )

    def own_copy(n):
        return pltpu.make_async_copy(left.at[n], left_in.at[n], left_recv.at[n])

    def prefix_copies(k, slot):
        to = {"region": lax.rem(me + k, regions)}
        return [
            pltpu.make_async_remote_copy(
                src_ref=src, dst_ref=dst.at[slot],
                send_sem=pre_send.at[i, k - 1], recv_sem=pre_recv.at[i, k - 1],
                device_id=to, device_id_type=MESH,
            )
            for i, (src, dst) in enumerate(((decay, decay_all), (energy, energy_all)))
        ]

    for k in range(1, regions):
        for copy in prefix_copies(k, me):
            copy.start()

    @pl.when(me < regions - 1)
    def _():
        for n in range(slots):
            left_copy(n).start()

    @pl.when(me == 0)
    def _():
        for n in range(slots):
            own_copy(n).start()

    live_slots = live[...]
    part[...] = jnp.zeros_like(part)

    lines[...] = operator[...].astype(F32)

    def where_one(test):
        return jnp.where(test, 1.0, 0.0).astype(BF16)

    def grid_of(shape):
        return [lax.broadcasted_iota(jnp.int32, shape, i) for i in range(2)]

    def spread_operator(out, swap):
        r, c = grid_of((side, chan * phys))
        u = (r // group) % chan
        if swap:
            u = u + 1 - 2 * (u % 2)
        pick_row = where_one((c // phys == u) & (c % phys == r // (chan * group)))
        r, c = grid_of((chan, side))
        total = jnp.zeros((side, side), F32)
        for t in range(phys):
            tall = jnp.dot(
                pick_row,
                lines[pl.ds(t, chan * phys, stride=phys), :].astype(BF16),
                preferred_element_type=F32,
            ).astype(BF16)
            pick_column = where_one((c // TILE == r) & (c % phys == t))
            total = total + jnp.dot(tall, pick_column, preferred_element_type=F32)
        r, c = grid_of((side, side))
        out[...] = jnp.where(r % group == (c // phys) % group, total, 0.0).astype(BF16)

    spread_operator(spread, False)
    spread_operator(flipped, True)

    def sum8(value):
        return jnp.sum(value.reshape(-1, 8, value.shape[-1]), axis=0)

    def spread_sum(total):
        return jnp.broadcast_to(jnp.sum(total, keepdims=True).reshape(1, 1), (1, blk))

    def length_of(square, whole):
        square = jnp.maximum(square, 1e-10 * whole)
        inverse = jnp.where(square > 0, lax.rsqrt(jnp.where(square > 0, square, 1.0)), 0.0)
        return square * inverse, inverse

    def share_of(value, norm):
        return jnp.where(norm > 0, value / jnp.where(norm > 0, norm, 1.0), 0.0)

    zero = jnp.zeros((8, blk), F32)
    lane = lax.broadcasted_iota(jnp.int32, (1, blk), 1)
    lane8 = lax.broadcasted_iota(jnp.int32, (8, blk), 1)
    chunk = 64

    def open_slot(n, p, vector, basis, norms):
        pltpu.make_async_copy(right.at[n], right_in.at[n], right_sem.at[n]).wait()
        pltpu.make_async_copy(start.at[n], start_in.at[n], start_sem.at[n]).wait()
        alive = jnp.broadcast_to(jnp.where(n < live_slots, 1.0, 0.0), (1, blk)).astype(F32)
        total = zero
        for r in range(0, wide, chunk):
            first = start_in[n, r : r + chunk].astype(F32) * alive
            basis[p, 0, r : r + chunk] = first
            vector[r : r + chunk] = first.astype(BF16)
            total = total + sum8(first * first)
            for i in range(1, STEPS):
                basis[p, i, r : r + chunk] = jnp.zeros((chunk, blk), F32)
        total = spread_sum(total)
        norms[...] = zero
        norms[0:1] = total
        part[STEPS] = jnp.where(lane8 == mine * slots + n, total, part[STEPS])

    def contract(n, vector, inner, mixed):
        half = wide // 2
        low_rows = lax.broadcasted_iota(jnp.int32, (side, 2 * blk), 0) % (2 * group) < group
        for h in range(2):
            rows = vector[h * half : (h + 1) * half]
            for w in range(0, chan, 2):
                side_by_side = jnp.concatenate([right_in[n, w], right_in[n, w + 1]], axis=1)
                inner[h * half : (h + 1) * half, w * blk : (w + 2) * blk] = jnp.dot(
                    rows, side_by_side, preferred_element_type=F32
                ).astype(BF16)
            for q in range(h * half // (4 * TILE), (h + 1) * half // (4 * TILE)):

                def stacked(g):
                    row = (4 * q + g) * TILE
                    return jnp.concatenate(
                        [inner[row : row + TILE, w * blk : (w + 1) * blk] for w in range(chan)], axis=0
                    )

                even = jnp.dot(
                    spread[...], jnp.concatenate([stacked(0), stacked(2)], axis=1),
                    preferred_element_type=F32,
                )
                odd = jnp.dot(
                    flipped[...], jnp.concatenate([stacked(1), stacked(3)], axis=1),
                    preferred_element_type=F32,
                )
                low = jnp.where(low_rows, even, odd)
                high = jnp.where(low_rows, odd, even)
                for s in range(phys):
                    for m in range(chan // 2):
                        row = s * chan * group + m * 2 * group
                        for k, tile in enumerate((low, high)):
                            tile = tile[row : row + 2 * group]
                            if k:
                                tile = pltpu.roll(tile, group, 0)
                            tile = jnp.concatenate([tile[:, :blk], tile[:, blk:]], axis=0).astype(BF16)
                            at = (2 * m + k) * blk + q * TILE
                            mixed[at : at + TILE, s * blk : (s + 1) * blk] = tile

    def close(n, p, j, vector, mixed, value, basis, norms):
        rows = jnp.concatenate([left_in[n, u] for u in range(chan)], axis=1)
        result = jnp.dot(rows, mixed[...], preferred_element_type=F32)
        for s in range(phys):
            value[pl.ds(s, blk, stride=phys), :] = result[:, s * blk : (s + 1) * blk]
        along, whole = [zero] * STEPS, zero
        for r in range(0, wide, chunk):
            image = value[r : r + chunk] + column[n, r : r + chunk] * vector[r : r + chunk].astype(F32)
            value[r : r + chunk] = image
            whole = whole + sum8(image * image)
            for i in range(STEPS):
                along[i] = along[i] + sum8(basis[p, i, r : r + chunk] * image)
        along, whole = [spread_sum(a) for a in along], spread_sum(whole)
        shares = [share_of(a, norms[i : i + 1]) for i, a in enumerate(along)]
        square = whole
        for a, c in zip(along, shares):
            square = square - a * c
        length, inverse = length_of(square, whole)
        cross, norm = [zero] * STEPS, zero
        for r in range(0, wide, chunk):
            bases = [basis[p, i, r : r + chunk] for i in range(STEPS)]
            probe = value[r : r + chunk]
            for c, b in zip(shares, bases):
                probe = probe - c * b
            probe = probe * inverse
            vector[r : r + chunk] = probe.astype(BF16)
            basis[p, j + 1, r : r + chunk] = probe
            norm = norm + sum8(probe * probe)
            for i, b in enumerate(bases):
                cross[i] = cross[i] + sum8(b * probe)
        norm = spread_sum(norm)
        line = lax.broadcasted_iota(jnp.int32, (8, blk), 0)
        norms[...] = jnp.where(line == j + 1, norm, norms[...])
        numbers = [*shares, length, *[spread_sum(c) for c in cross], norm]
        tile = zero
        for i, number in enumerate(numbers):
            tile = jnp.where(line == i, number, tile)
        part[j] = jnp.where(lane8 == mine * slots + n, tile, part[j])

    open_slot(0, 0, vector_a, basis_a, norms_a)
    open_slot(1, 0, vector_b, basis_b, norms_b)
    contract(0, vector_a, inner_a, mixed_a)

    decay_all[me] = decay[...]
    energy_all[me] = energy[...]
    for k in range(1, regions):
        for copy in prefix_copies(k, lax.rem(me + regions - k, regions)):
            copy.wait()
    offsets = jnp.zeros((slots, blk), F32)
    for p in range(regions - 1):
        offsets = jnp.where(p < me, decay_all[p] * offsets + energy_all[p], offsets)
    for n in range(slots):
        turned = jnp.broadcast_to(offsets[n : n + 1], (blk, blk)).T
        for s in range(phys):
            column[n, pl.ds(s, blk, stride=phys), :] = turned

    def turn(i, carry):
        p, j = i // STEPS, i % STEPS
        n = 2 * p
        after = (i + 1) % rounds

        @pl.when(j == 0)
        def _():
            own_copy(n).wait()

        close(n, p, j, vector_a, mixed_a, value_a, basis_a, norms_a)
        contract(n + 1, vector_b, inner_b, mixed_b)

        @pl.when(j == 0)
        def _():
            own_copy(n + 1).wait()

        @pl.when((j == STEPS - 1) & (i + 1 < rounds))
        def _():
            open_slot(n + 2, p + 1, vector_a, basis_a, norms_a)

        close(n + 1, p, j, vector_b, mixed_b, value_b, basis_b, norms_b)
        contract(2 * (after // STEPS), vector_a, inner_a, mixed_a)

        @pl.when((j == STEPS - 1) & (i + 1 < rounds))
        def _():
            open_slot(n + 3, p + 1, vector_b, basis_b, norms_b)

        return carry

    lax.fori_loop(0, rounds, turn, 0)

    gathered[mine] = part[...]

    def copy_of(k, slot):
        return pltpu.make_async_remote_copy(
            src_ref=part, dst_ref=gathered.at[slot],
            send_sem=sum_send.at[k - 1], recv_sem=sum_recv.at[k - 1],
            device_id={"sector": lax.rem(mine + k, sectors)}, device_id_type=MESH,
        )

    for k in range(1, sectors):
        copy_of(k, mine).start()
    for k in range(1, sectors):
        copy_of(k, lax.rem(mine + sectors - k, sectors)).wait()
    table = gathered[0]
    for i in range(1, sectors):
        table = table + gathered[i]
    images = [[table[j, i : i + 1] for i in range(STEPS)] + [None] for j in range(STEPS)]
    gram = {(0, 0): table[STEPS, 0:1]}
    for j in range(STEPS):
        length = table[j, STEPS : STEPS + 1]
        images[j] = [c if i <= j else None for i, c in enumerate(images[j])]
        images[j][j + 1] = length
        for i in range(j + 1):
            gram[i, j + 1] = table[j, STEPS + 1 + i : STEPS + 2 + i]
        gram[j + 1, j + 1] = table[j, 2 * STEPS + 1 : 2 * STEPS + 2]

    def inner(x, y):
        total = jnp.zeros((1, blk), F32)
        for i, xi in enumerate(x):
            for j, yj in enumerate(y):
                if xi is not None and yj is not None:
                    total = total + xi * yj * gram[min(i, j), max(i, j)]
        return jnp.broadcast_to(jnp.sum(total, axis=1, keepdims=True), (1, blk))

    def mix(p, x, q, y):
        def one(a, b):
            if a is None:
                return None if b is None else q * b
            return p * a if b is None else p * a + q * b

        return [one(a, b) for a, b in zip(x, y)]

    unit = jnp.ones((1, blk), F32)
    inverse = lax.rsqrt(inner([unit], [unit]) + EPS)
    current = [inverse * unit, None, None, None]
    applied = [inverse * a if a is not None else None for a in images[0]]
    for _ in range(DAV):
        quotient = inner(current, applied)
        residual = mix(1.0, applied, -quotient, current)
        resid_sq = inner(residual, residual)
        factor = lax.rsqrt(resid_sq + EPS)
        search = [factor * a if a is not None else None for a in residual]
        moved = [None] * (STEPS + 1)
        for a, line in zip(search, images):
            if a is not None:
                moved = mix(1.0, moved, a, line)
        curvature = inner(search, moved)
        cos_part, sin_part = half_rotation(-2.0 * resid_sq * factor, curvature - quotient)
        current = mix(cos_part, current, sin_part, search)
        applied = mix(cos_part, applied, sin_part, moved)
    energy_out[...] = jnp.broadcast_to(inner(current, applied), (8, blk))
    scale = math.sqrt(slots * sectors * blk * phys * blk)

    for n in range(slots):
        here = lane == mine * slots + n
        basis = (basis_a, basis_b)[n % 2]
        factors = [
            jnp.broadcast_to(jnp.sum(jnp.where(here, scale * c, 0.0), axis=1, keepdims=True), (1, blk))
            for c in current[:STEPS]
        ]
        for r in range(0, wide, chunk):
            state = jnp.zeros((chunk, blk), F32)
            for i, c in enumerate(factors):
                state = state + c * basis[n // 2, i, r : r + chunk]
            state_out[n, r : r + chunk] = state.astype(BF16)

    @pl.when(me < regions - 1)
    def _():
        for n in range(slots):
            left_copy(n).wait_send()


def finish(state, energy, out, density, energy_out, rows_buf, density_buf, sems):
    slots, wide, blk = state.shape
    phys = wide // blk
    copies = [pltpu.make_async_copy(state, out, sems.at[slots])]
    copies[0].start()
    for n in range(slots):
        rows_buf[n] = state[n].astype(F32)
        total = jnp.zeros((blk, blk), F32)
        for s in range(phys):
            rows = rows_buf[n, pl.ds(s, blk, stride=phys), :].astype(BF16)
            total = total + lax.dot_general(
                rows, rows, (((1,), (1,)), ((), ())), preferred_element_type=F32
            )
        density_buf[n] = total / (phys * blk)
        copies.append(pltpu.make_async_copy(density_buf.at[n], density.at[n], sems.at[n]))
        copies[-1].start()
    energy_out[0] = energy[0, 0]
    for copy in copies:
        copy.wait()


def body(regions, sectors, start_state, left_env, right_env, mpo_tensor, decay, energy_terms, live_count):
    _, slots, blk, phys, _ = start_state.shape
    chan = left_env.shape[2]
    wide = phys * blk
    side = chan * TILE
    vmem = pl.BlockSpec(memory_space=pltpu.VMEM)
    hbm = pl.BlockSpec(memory_space=pl.ANY)
    smem = pl.BlockSpec(memory_space=pltpu.SMEM)
    dma = pltpu.SemaphoreType.DMA
    twice = lambda *spec: [pltpu.VMEM(*spec)] * 2
    outs = pl.pallas_call(
        functools.partial(kernel, regions, sectors),
        out_shape=(
            jax.ShapeDtypeStruct((slots, wide, blk), BF16),
            jax.ShapeDtypeStruct((8, blk), F32),
        ),
        in_specs=[hbm, hbm, hbm, vmem, vmem, vmem, vmem],
        out_specs=(vmem, vmem),
        scratch_shapes=[
            pltpu.VMEM((slots, wide, blk), BF16),
            pltpu.VMEM((slots, chan, blk, blk), BF16),
            pltpu.VMEM((slots, chan, blk, blk), BF16),
            pltpu.VMEM((chan * phys * phys, chan), F32),
            *twice((side, side), BF16),
            pltpu.VMEM((slots, wide, blk), F32),
            *twice((wide, blk), BF16),
            *twice((wide, chan * blk), BF16),
            *twice((chan * blk, wide), BF16),
            *twice((wide, blk), F32),
            *twice((slots // 2, STEPS + 1, wide, blk), F32),
            *twice((8, blk), F32),
            pltpu.VMEM((regions, slots, blk), F32),
            pltpu.VMEM((regions, slots, blk), F32),
            pltpu.VMEM((STEPS + 1, 8, blk), F32),
            pltpu.VMEM((sectors, STEPS + 1, 8, blk), F32),
            dma((slots,)), dma((slots,)), dma((slots,)), dma((slots,)),
            dma((2, regions)), dma((2, regions)),
            dma((sectors,)), dma((sectors,)),
        ],
        compiler_params=pltpu.CompilerParams(
            collective_id=0, has_side_effects=True, vmem_limit_bytes=48 * 2**20
        ),
    )(
        start_state.reshape(slots, wide, blk), left_env[0], right_env[0],
        mpo_tensor.reshape(chan * phys * phys, chan),
        decay[0], energy_terms[0], live_count,
    )
    state_out, density, energy = pl.pallas_call(
        finish,
        out_shape=(
            jax.ShapeDtypeStruct((slots, wide, blk), BF16),
            jax.ShapeDtypeStruct((slots, blk, blk), F32),
            jax.ShapeDtypeStruct((1,), F32),
        ),
        in_specs=[vmem, vmem],
        out_specs=(hbm, hbm, smem),
        scratch_shapes=[
            pltpu.VMEM((slots, wide, blk), F32),
            pltpu.VMEM((slots, blk, blk), F32),
            dma((slots + 1,)),
        ],
    )(*outs)
    return (
        state_out.reshape(start_state.shape),
        density.reshape(1, slots, blk, blk),
        energy,
    )


def solution(mesh):
    in_specs = (
        P("region", "sector", None, None, None),
        P("region", "sector", None, None, None),
        P("region", "sector", None, None, None),
        P(),
        P("region", "sector", None),
        P("region", "sector", None),
        P("region", "sector"),
    )
    out_specs = (
        P("region", "sector", None, None, None),
        P("region", "sector", None, None),
        P("region"),
    )
    step = functools.partial(body, mesh.shape["region"], mesh.shape["sector"])
    return jax.shard_map(step, mesh=mesh, in_specs=in_specs, out_specs=out_specs, check_vma=False)
```

```python
import functools
import math

import jax
import jax.numpy as jnp
from jax import lax
from jax.experimental import pallas as pl
from jax.experimental.pallas import tpu as pltpu
from jax.sharding import PartitionSpec as P

DAV = 2
EPS = 1e-06
MESH = pl.DeviceIdType.MESH
F32 = jnp.float32
BF16 = jnp.bfloat16
STEPS = DAV + 1
TILE = 16


def half_rotation(y, x):
    top = jnp.maximum(jnp.abs(x), jnp.abs(y))
    safe = jnp.where(top > 0, top, 1.0)
    xn, yn = x / safe, y / safe
    h = jnp.sqrt(xn * xn + yn * yn)
    h = jnp.where(top > 0, h, 1.0)
    big = jnp.sqrt(0.5 * (h + jnp.abs(xn)) / h)
    small = jnp.abs(yn) / (2.0 * h * big)
    big = jnp.where(top > 0, big, 1.0)
    small = jnp.where(top > 0, small, 0.0)
    cos_part = jnp.where(x >= 0, big, small)
    sin_size = jnp.where(x >= 0, small, big)
    return cos_part, jnp.where(y > 0, sin_size, -sin_size)


def kernel(
    regions, sectors, start, left, right, operator, decay, energy, live,
    state_out, energy_out,
    start_in, left_in, right_in, lines, spread, flipped, column,
    vector_a, vector_b, inner_a, inner_b, mixed_a, mixed_b, value_a, value_b,
    basis_a, basis_b, norms_a, norms_b, decay_all, energy_all, part, gathered,
    left_send, left_recv, right_sem, start_sem, pre_send, pre_recv, sum_send, sum_recv,
):
    slots, chan, blk, _ = left.shape
    wide = start.shape[1]
    phys = wide // blk
    me, mine = lax.axis_index("region"), lax.axis_index("sector")
    group = TILE // phys
    side = chan * TILE
    pairs = slots // 2
    rounds = pairs * STEPS
    for n in range(slots):
        pltpu.make_async_copy(right.at[n], right_in.at[n], right_sem.at[n]).start()
        pltpu.make_async_copy(start.at[n], start_in.at[n], start_sem.at[n]).start()

    barrier = pltpu.get_barrier_semaphore()
    for k in range(1, regions):
        pl.semaphore_signal(
            barrier, 1, device_id={"region": lax.rem(me + k, regions)}, device_id_type=MESH
        )
    for k in range(1, sectors):
        pl.semaphore_signal(
            barrier, 1, device_id={"sector": lax.rem(mine + k, sectors)}, device_id_type=MESH
        )
    pl.semaphore_wait(barrier, regions + sectors - 2)

    def left_copy(n):
        return pltpu.make_async_remote_copy(
            src_ref=left.at[n], dst_ref=left_in.at[n],
            send_sem=left_send.at[n], recv_sem=left_recv.at[n],
            device_id={"region": lax.rem(me + 1, regions)}, device_id_type=MESH,
        )

    def own_copy(n):
        return pltpu.make_async_copy(left.at[n], left_in.at[n], left_recv.at[n])

    def prefix_copies(k, slot):
        to = {"region": lax.rem(me + k, regions)}
        return [
            pltpu.make_async_remote_copy(
                src_ref=src, dst_ref=dst.at[slot],
                send_sem=pre_send.at[i, k - 1], recv_sem=pre_recv.at[i, k - 1],
                device_id=to, device_id_type=MESH,
            )
            for i, (src, dst) in enumerate(((decay, decay_all), (energy, energy_all)))
        ]

    for k in range(1, regions):
        for copy in prefix_copies(k, me):
            copy.start()

    @pl.when(me < regions - 1)
    def _():
        for n in range(slots):
            left_copy(n).start()

    @pl.when(me == 0)
    def _():
        for n in range(slots):
            own_copy(n).start()

    live_slots = live[...]
    part[...] = jnp.zeros_like(part)

    lines[...] = operator[...].astype(F32)

    def where_one(test):
        return jnp.where(test, 1.0, 0.0).astype(BF16)

    def grid_of(shape):
        return [lax.broadcasted_iota(jnp.int32, shape, i) for i in range(2)]

    def spread_operator(out, swap):
        r, c = grid_of((side, chan * phys))
        u = (r // group) % chan
        if swap:
            u = u + 1 - 2 * (u % 2)
        pick_row = where_one((c // phys == u) & (c % phys == r // (chan * group)))
        r, c = grid_of((chan, side))
        total = jnp.zeros((side, side), F32)
        for t in range(phys):
            tall = jnp.dot(
                pick_row,
                lines[pl.ds(t, chan * phys, stride=phys), :].astype(BF16),
                preferred_element_type=F32,
            ).astype(BF16)
            pick_column = where_one((c // TILE == r) & (c % phys == t))
            total = total + jnp.dot(tall, pick_column, preferred_element_type=F32)
        r, c = grid_of((side, side))
        out[...] = jnp.where(r % group == (c // phys) % group, total, 0.0).astype(BF16)

    spread_operator(spread, False)
    spread_operator(flipped, True)

    def sum8(value):
        return jnp.sum(value.reshape(-1, 8, value.shape[-1]), axis=0)

    def spread_sum(total):
        return jnp.broadcast_to(jnp.sum(total, keepdims=True).reshape(1, 1), (1, blk))

    def length_of(square, whole):
        square = jnp.maximum(square, 1e-10 * whole)
        inverse = jnp.where(square > 0, lax.rsqrt(jnp.where(square > 0, square, 1.0)), 0.0)
        return square * inverse, inverse

    def share_of(value, norm):
        return jnp.where(norm > 0, value / jnp.where(norm > 0, norm, 1.0), 0.0)

    zero = jnp.zeros((8, blk), F32)
    lane = lax.broadcasted_iota(jnp.int32, (1, blk), 1)
    lane8 = lax.broadcasted_iota(jnp.int32, (8, blk), 1)
    line8 = lax.broadcasted_iota(jnp.int32, (8, blk), 0)
    chunk = 64

    def open_slot(n, p, vector, basis, norms):
        pltpu.make_async_copy(right.at[n], right_in.at[n], right_sem.at[n]).wait()
        pltpu.make_async_copy(start.at[n], start_in.at[n], start_sem.at[n]).wait()
        alive = jnp.broadcast_to(jnp.where(n < live_slots, 1.0, 0.0), (1, blk)).astype(F32)
        total = zero
        for r in range(0, wide, chunk):
            first = start_in[n, r : r + chunk].astype(F32) * alive
            basis[p, 0, r : r + chunk] = first
            vector[r : r + chunk] = first.astype(BF16)
            total = total + sum8(first * first)
            for i in range(1, STEPS):
                basis[p, i, r : r + chunk] = jnp.zeros((chunk, blk), F32)
        total = spread_sum(total)
        norms[...] = zero
        norms[0:1] = total
        part[...] = jnp.where((line8 == n) & (lane8 == 8 * STEPS), total, part[...])

    def contract(n, vector, inner, mixed):
        half = wide // 2
        low_rows = lax.broadcasted_iota(jnp.int32, (side, 2 * blk), 0) % (2 * group) < group
        for h in range(2):
            rows = vector[h * half : (h + 1) * half]
            for w in range(0, chan, 2):
                side_by_side = jnp.concatenate([right_in[n, w], right_in[n, w + 1]], axis=1)
                inner[h * half : (h + 1) * half, w * blk : (w + 2) * blk] = jnp.dot(
                    rows, side_by_side, preferred_element_type=F32
                ).astype(BF16)
            for q in range(h * half // (4 * TILE), (h + 1) * half // (4 * TILE)):

                def stacked(g):
                    row = (4 * q + g) * TILE
                    return jnp.concatenate(
                        [inner[row : row + TILE, w * blk : (w + 1) * blk] for w in range(chan)], axis=0
                    )

                even = jnp.dot(
                    spread[...], jnp.concatenate([stacked(0), stacked(2)], axis=1),
                    preferred_element_type=F32,
                )
                odd = jnp.dot(
                    flipped[...], jnp.concatenate([stacked(1), stacked(3)], axis=1),
                    preferred_element_type=F32,
                )
                low = jnp.where(low_rows, even, odd)
                high = jnp.where(low_rows, odd, even)
                for s in range(phys):
                    for m in range(chan // 2):
                        row = s * chan * group + m * 2 * group
                        for k, tile in enumerate((low, high)):
                            tile = tile[row : row + 2 * group]
                            if k:
                                tile = pltpu.roll(tile, group, 0)
                            tile = jnp.concatenate([tile[:, :blk], tile[:, blk:]], axis=0).astype(BF16)
                            at = (2 * m + k) * blk + q * TILE
                            mixed[at : at + TILE, s * blk : (s + 1) * blk] = tile

    def close(n, p, j, vector, mixed, value, basis, norms):
        rows = jnp.concatenate([left_in[n, u] for u in range(chan)], axis=1)
        result = jnp.dot(rows, mixed[...], preferred_element_type=F32)
        for s in range(phys):
            value[pl.ds(s, blk, stride=phys), :] = result[:, s * blk : (s + 1) * blk]
        along, whole = [zero] * STEPS, zero
        for r in range(0, wide, chunk):
            image = value[r : r + chunk] + column[n, r : r + chunk] * vector[r : r + chunk].astype(F32)
            value[r : r + chunk] = image
            whole = whole + sum8(image * image)
            for i in range(STEPS):
                along[i] = along[i] + sum8(basis[p, i, r : r + chunk] * image)
        along, whole = [spread_sum(a) for a in along], spread_sum(whole)
        shares = [share_of(a, norms[i : i + 1]) for i, a in enumerate(along)]
        square = whole
        for a, c in zip(along, shares):
            square = square - a * c
        length, inverse = length_of(square, whole)
        cross, norm = [zero] * STEPS, zero
        for r in range(0, wide, chunk):
            bases = [basis[p, i, r : r + chunk] for i in range(STEPS)]
            probe = value[r : r + chunk]
            for c, b in zip(shares, bases):
                probe = probe - c * b
            probe = probe * inverse
            vector[r : r + chunk] = probe.astype(BF16)
            basis[p, j + 1, r : r + chunk] = probe
            norm = norm + sum8(probe * probe)
            for i, b in enumerate(bases):
                cross[i] = cross[i] + sum8(b * probe)
        norm = spread_sum(norm)
        norms[...] = jnp.where(line8 == j + 1, norm, norms[...])
        numbers = [*shares, length, *[spread_sum(c) for c in cross], norm]
        row = jnp.zeros((1, blk), F32)
        for i, number in enumerate(numbers):
            row = jnp.where(lane == 8 * j + i, number, row)
        part[...] = jnp.where((line8 == n) & (lane8 // 8 == j), row, part[...])

    open_slot(0, 0, vector_a, basis_a, norms_a)
    open_slot(1, 0, vector_b, basis_b, norms_b)
    contract(0, vector_a, inner_a, mixed_a)

    decay_all[me] = decay[...]
    energy_all[me] = energy[...]
    for k in range(1, regions):
        for copy in prefix_copies(k, lax.rem(me + regions - k, regions)):
            copy.wait()
    offsets = jnp.zeros((slots, blk), F32)
    for p in range(regions - 1):
        offsets = jnp.where(p < me, decay_all[p] * offsets + energy_all[p], offsets)
    for n in range(slots):
        turned = jnp.broadcast_to(offsets[n : n + 1], (blk, blk)).T
        for s in range(phys):
            column[n, pl.ds(s, blk, stride=phys), :] = turned

    def turn(i, carry):
        p, j = i // STEPS, i % STEPS
        n = 2 * p
        after = (i + 1) % rounds

        @pl.when(j == 0)
        def _():
            own_copy(n).wait()

        close(n, p, j, vector_a, mixed_a, value_a, basis_a, norms_a)
        contract(n + 1, vector_b, inner_b, mixed_b)

        @pl.when(j == 0)
        def _():
            own_copy(n + 1).wait()

        @pl.when((j == STEPS - 1) & (i + 1 < rounds))
        def _():
            open_slot(n + 2, p + 1, vector_a, basis_a, norms_a)

        close(n + 1, p, j, vector_b, mixed_b, value_b, basis_b, norms_b)
        contract(2 * (after // STEPS), vector_a, inner_a, mixed_a)

        @pl.when((j == STEPS - 1) & (i + 1 < rounds))
        def _():
            open_slot(n + 3, p + 1, vector_b, basis_b, norms_b)

        return carry

    lax.fori_loop(0, rounds, turn, 0)

    gathered[mine] = part[...]

    def copy_of(k, slot):
        return pltpu.make_async_remote_copy(
            src_ref=part, dst_ref=gathered.at[slot],
            send_sem=sum_send.at[k - 1], recv_sem=sum_recv.at[k - 1],
            device_id={"sector": lax.rem(mine + k, sectors)}, device_id_type=MESH,
        )

    for k in range(1, sectors):
        copy_of(k, mine).start()
    for k in range(1, sectors):
        copy_of(k, lax.rem(mine + sectors - k, sectors)).wait()
    many = sectors * 8
    table = gathered[...].reshape(many, blk).T
    images = [[table[8 * j + i : 8 * j + i + 1] for i in range(STEPS)] + [None] for j in range(STEPS)]
    gram = {(0, 0): table[8 * STEPS : 8 * STEPS + 1]}
    for j in range(STEPS):
        length = table[8 * j + STEPS : 8 * j + STEPS + 1]
        images[j] = [c if i <= j else None for i, c in enumerate(images[j])]
        images[j][j + 1] = length
        for i in range(j + 1):
            gram[i, j + 1] = table[8 * j + STEPS + 1 + i : 8 * j + STEPS + 2 + i]
        gram[j + 1, j + 1] = table[8 * j + 2 * STEPS + 1 : 8 * j + 2 * STEPS + 2]

    def inner(x, y):
        total = jnp.zeros((1, many), F32)
        for i, xi in enumerate(x):
            for j, yj in enumerate(y):
                if xi is not None and yj is not None:
                    total = total + xi * yj * gram[min(i, j), max(i, j)]
        return jnp.broadcast_to(jnp.sum(total, axis=1, keepdims=True), (1, many))

    def mix(p, x, q, y):
        def one(a, b):
            if a is None:
                return None if b is None else q * b
            return p * a if b is None else p * a + q * b

        return [one(a, b) for a, b in zip(x, y)]

    unit = jnp.ones((1, many), F32)
    inverse = lax.rsqrt(inner([unit], [unit]) + EPS)
    current = [inverse * unit, None, None, None]
    applied = [inverse * a if a is not None else None for a in images[0]]
    for _ in range(DAV):
        quotient = inner(current, applied)
        residual = mix(1.0, applied, -quotient, current)
        resid_sq = inner(residual, residual)
        factor = lax.rsqrt(resid_sq + EPS)
        search = [factor * a if a is not None else None for a in residual]
        moved = [None] * (STEPS + 1)
        for a, line in zip(search, images):
            if a is not None:
                moved = mix(1.0, moved, a, line)
        curvature = inner(search, moved)
        cos_part, sin_part = half_rotation(-2.0 * resid_sq * factor, curvature - quotient)
        current = mix(cos_part, current, sin_part, search)
        applied = mix(cos_part, applied, sin_part, moved)
    energy_out[...] = jnp.broadcast_to(inner(current, applied)[:, :1], (8, blk))
    scale = math.sqrt(slots * sectors * blk * phys * blk)

    for n in range(slots):
        here = lax.broadcasted_iota(jnp.int32, (1, many), 1) == mine * 8 + n
        basis = (basis_a, basis_b)[n % 2]
        factors = [
            jnp.broadcast_to(jnp.sum(jnp.where(here, scale * c, 0.0), axis=1, keepdims=True), (1, blk))
            for c in current[:STEPS]
        ]
        for r in range(0, wide, chunk):
            state = jnp.zeros((chunk, blk), F32)
            for i, c in enumerate(factors):
                state = state + c * basis[n // 2, i, r : r + chunk]
            state_out[n, r : r + chunk] = state.astype(BF16)

    @pl.when(me < regions - 1)
    def _():
        for n in range(slots):
            left_copy(n).wait_send()


def finish(state, energy, out, density, energy_out, rows_buf, density_buf, sems):
    slots, wide, blk = state.shape
    phys = wide // blk
    copies = [pltpu.make_async_copy(state, out, sems.at[slots])]
    copies[0].start()
    for n in range(slots):
        rows_buf[n] = state[n].astype(F32)
        total = jnp.zeros((blk, blk), F32)
        for s in range(phys):
            rows = rows_buf[n, pl.ds(s, blk, stride=phys), :].astype(BF16)
            total = total + lax.dot_general(
                rows, rows, (((1,), (1,)), ((), ())), preferred_element_type=F32
            )
        density_buf[n] = total / (phys * blk)
        copies.append(pltpu.make_async_copy(density_buf.at[n], density.at[n], sems.at[n]))
        copies[-1].start()
    energy_out[0] = energy[0, 0]
    for copy in copies:
        copy.wait()


def body(regions, sectors, start_state, left_env, right_env, mpo_tensor, decay, energy_terms, live_count):
    _, slots, blk, phys, _ = start_state.shape
    chan = left_env.shape[2]
    wide = phys * blk
    side = chan * TILE
    vmem = pl.BlockSpec(memory_space=pltpu.VMEM)
    hbm = pl.BlockSpec(memory_space=pltpu.HBM)
    smem = pl.BlockSpec(memory_space=pltpu.SMEM)
    dma = pltpu.SemaphoreType.DMA
    twice = lambda *spec: [pltpu.VMEM(*spec)] * 2
    outs = pl.pallas_call(
        functools.partial(kernel, regions, sectors),
        out_shape=(
            jax.ShapeDtypeStruct((slots, wide, blk), BF16),
            jax.ShapeDtypeStruct((8, blk), F32),
        ),
        in_specs=[hbm, hbm, hbm, vmem, vmem, vmem, vmem],
        out_specs=(vmem, vmem),
        scratch_shapes=[
            pltpu.VMEM((slots, wide, blk), BF16),
            pltpu.VMEM((slots, chan, blk, blk), BF16),
            pltpu.VMEM((slots, chan, blk, blk), BF16),
            pltpu.VMEM((chan * phys * phys, chan), F32),
            *twice((side, side), BF16),
            pltpu.VMEM((slots, wide, blk), F32),
            *twice((wide, blk), BF16),
            *twice((wide, chan * blk), BF16),
            *twice((chan * blk, wide), BF16),
            *twice((wide, blk), F32),
            *twice((slots // 2, STEPS + 1, wide, blk), F32),
            *twice((8, blk), F32),
            pltpu.VMEM((regions, slots, blk), F32),
            pltpu.VMEM((regions, slots, blk), F32),
            pltpu.VMEM((8, blk), F32),
            pltpu.VMEM((sectors, 8, blk), F32),
            dma((slots,)), dma((slots,)), dma((slots,)), dma((slots,)),
            dma((2, regions)), dma((2, regions)),
            dma((sectors,)), dma((sectors,)),
        ],
        compiler_params=pltpu.CompilerParams(
            collective_id=0, has_side_effects=True, vmem_limit_bytes=48 * 2**20
        ),
    )(
        start_state.reshape(slots, wide, blk), left_env[0], right_env[0],
        mpo_tensor.reshape(chan * phys * phys, chan),
        decay[0], energy_terms[0], live_count,
    )
    state_out, density, energy = pl.pallas_call(
        finish,
        out_shape=(
            jax.ShapeDtypeStruct((slots, wide, blk), BF16),
            jax.ShapeDtypeStruct((slots, blk, blk), F32),
            jax.ShapeDtypeStruct((1,), F32),
        ),
        in_specs=[vmem, vmem],
        out_specs=(hbm, hbm, smem),
        scratch_shapes=[
            pltpu.VMEM((slots, wide, blk), F32),
            pltpu.VMEM((slots, blk, blk), F32),
            dma((slots + 1,)),
        ],
    )(*outs)
    return (
        state_out.reshape(start_state.shape),
        density.reshape(1, slots, blk, blk),
        energy,
    )


def solution(mesh):
    in_specs = (
        P("region", "sector", None, None, None),
        P("region", "sector", None, None, None),
        P("region", "sector", None, None, None),
        P(),
        P("region", "sector", None),
        P("region", "sector", None),
        P("region", "sector"),
    )
    out_specs = (
        P("region", "sector", None, None, None),
        P("region", "sector", None, None),
        P("region"),
    )
    step = functools.partial(body, mesh.shape["region"], mesh.shape["sector"])
    return jax.shard_map(step, mesh=mesh, in_specs=in_specs, out_specs=out_specs, check_vma=False)
```

```python
import functools
import math

import jax
import jax.numpy as jnp
from jax import lax
from jax.experimental import pallas as pl
from jax.experimental.pallas import tpu as pltpu
from jax.sharding import PartitionSpec as P

DAV = 2
EPS = 1e-06
MESH = pl.DeviceIdType.MESH
F32 = jnp.float32
BF16 = jnp.bfloat16
STEPS = DAV + 1
TILE = 16


def half_rotation(y, x):
    top = jnp.maximum(jnp.abs(x), jnp.abs(y))
    safe = jnp.where(top > 0, top, 1.0)
    xn, yn = x / safe, y / safe
    h = jnp.sqrt(xn * xn + yn * yn)
    h = jnp.where(top > 0, h, 1.0)
    big = jnp.sqrt(0.5 * (h + jnp.abs(xn)) / h)
    small = jnp.abs(yn) / (2.0 * h * big)
    big = jnp.where(top > 0, big, 1.0)
    small = jnp.where(top > 0, small, 0.0)
    cos_part = jnp.where(x >= 0, big, small)
    sin_size = jnp.where(x >= 0, small, big)
    return cos_part, jnp.where(y > 0, sin_size, -sin_size)


def kernel(
    regions, sectors, start, left, right, operator, decay, energy, live,
    state_out, energy_out,
    start_in, left_in, right_in, lines, spread, flipped, column,
    vector_a, vector_b, inner_a, inner_b, mixed_a, mixed_b, value_a, value_b,
    basis, norms, decay_all, energy_all, part, gathered,
    left_send, left_recv, right_sem, start_sem, pre_send, pre_recv, sum_send, sum_recv,
):
    slots, chan, blk, _ = left.shape
    wide = start.shape[1]
    phys = wide // blk
    me, mine = lax.axis_index("region"), lax.axis_index("sector")
    group = TILE // phys
    side = chan * TILE
    here_zero = me // regions
    crossing = (me > 0) & (me % 2 == 0)
    rounds = jnp.where(crossing, 0, slots // 2 * STEPS)
    singles = jnp.where(crossing, slots, 0)
    for n in range(slots):
        pltpu.make_async_copy(right.at[n], right_in.at[n], right_sem.at[n]).start()
        pltpu.make_async_copy(start.at[n], start_in.at[n], start_sem.at[n]).start()

    barrier = pltpu.get_barrier_semaphore()
    for k in range(1, regions):
        pl.semaphore_signal(
            barrier, 1, device_id={"region": lax.rem(me + k, regions)}, device_id_type=MESH
        )
    for k in range(1, sectors):
        pl.semaphore_signal(
            barrier, 1, device_id={"sector": lax.rem(mine + k, sectors)}, device_id_type=MESH
        )
    pl.semaphore_wait(barrier, regions + sectors - 2)

    def left_copy(n):
        return pltpu.make_async_remote_copy(
            src_ref=left.at[n], dst_ref=left_in.at[n],
            send_sem=left_send.at[n], recv_sem=left_recv.at[n],
            device_id={"region": lax.rem(me + 1, regions)}, device_id_type=MESH,
        )

    def own_copy(n):
        return pltpu.make_async_copy(left.at[n], left_in.at[n], left_recv.at[n])

    def prefix_copies(k, slot):
        to = {"region": lax.rem(me + k, regions)}
        return [
            pltpu.make_async_remote_copy(
                src_ref=src, dst_ref=dst.at[slot],
                send_sem=pre_send.at[i, k - 1], recv_sem=pre_recv.at[i, k - 1],
                device_id=to, device_id_type=MESH,
            )
            for i, (src, dst) in enumerate(((decay, decay_all), (energy, energy_all)))
        ]

    for k in range(1, regions):
        for copy in prefix_copies(k, me):
            copy.start()

    @pl.when(me < regions - 1)
    def _():
        for n in range(slots):
            left_copy(n).start()

    @pl.when(me == 0)
    def _():
        for n in range(slots):
            own_copy(n).start()

    live_slots = live[...]
    part[...] = jnp.zeros_like(part)

    lines[...] = operator[...].astype(F32)

    def where_one(test):
        return jnp.where(test, 1.0, 0.0).astype(BF16)

    def grid_of(shape):
        return [lax.broadcasted_iota(jnp.int32, shape, i) for i in range(2)]

    def spread_operator(out, swap):
        r, c = grid_of((side, chan * phys))
        u = (r // group) % chan
        if swap:
            u = u + 1 - 2 * (u % 2)
        pick_row = where_one((c // phys == u) & (c % phys == r // (chan * group)))
        r, c = grid_of((chan, side))
        total = jnp.zeros((side, side), F32)
        for t in range(phys):
            tall = jnp.dot(
                pick_row,
                lines[pl.ds(t, chan * phys, stride=phys), :].astype(BF16),
                preferred_element_type=F32,
            ).astype(BF16)
            pick_column = where_one((c // TILE == r) & (c % phys == t))
            total = total + jnp.dot(tall, pick_column, preferred_element_type=F32)
        r, c = grid_of((side, side))
        out[...] = jnp.where(r % group == (c // phys) % group, total, 0.0).astype(BF16)

    spread_operator(spread, False)
    spread_operator(flipped, True)

    def sum8(value):
        return jnp.sum(value.reshape(-1, 8, value.shape[-1]), axis=0)

    def spread_sum(total):
        return jnp.broadcast_to(jnp.sum(total, keepdims=True).reshape(1, 1), (1, blk))

    def length_of(square, whole):
        square = jnp.maximum(square, 1e-10 * whole)
        inverse = jnp.where(square > 0, lax.rsqrt(jnp.where(square > 0, square, 1.0)), 0.0)
        return square * inverse, inverse

    def share_of(value, norm):
        return jnp.where(norm > 0, value / jnp.where(norm > 0, norm, 1.0), 0.0)

    zero = jnp.zeros((8, blk), F32)
    lane = lax.broadcasted_iota(jnp.int32, (1, blk), 1)
    lane8 = lax.broadcasted_iota(jnp.int32, (8, blk), 1)
    line8 = lax.broadcasted_iota(jnp.int32, (8, blk), 0)
    chunk = 64

    def open_slot(n):
        pltpu.make_async_copy(right.at[n], right_in.at[n], right_sem.at[n]).wait()
        pltpu.make_async_copy(start.at[n], start_in.at[n], start_sem.at[n]).wait()
        alive = jnp.broadcast_to(jnp.where(n < live_slots, 1.0, 0.0), (1, blk)).astype(F32)
        total = zero
        for r in range(0, wide, chunk):
            first = start_in[n, r : r + chunk].astype(F32) * alive
            basis[n, 0, r : r + chunk] = first
            vector_a[n, r : r + chunk] = first.astype(BF16)
            vector_b[n, r : r + chunk] = first.astype(BF16)
            total = total + sum8(first * first)
            for i in range(1, STEPS):
                basis[n, i, r : r + chunk] = jnp.zeros((chunk, blk), F32)
        total = spread_sum(total)
        norms[n] = jnp.where(line8 == 0, total, 0.0)
        part[...] = jnp.where((line8 == n) & (lane8 == 8 * STEPS), total, part[...])

    low_rows = lax.broadcasted_iota(jnp.int32, (side, 2 * blk), 0) % (2 * group) < group

    def contract(n, vector, inner, mixed):
        half = wide // 2

        def right_part(h, w):
            side_by_side = jnp.concatenate([right_in[n, w], right_in[n, w + 1]], axis=1)
            inner[h * half : (h + 1) * half, w * blk : (w + 2) * blk] = jnp.dot(
                vector[n, h * half : (h + 1) * half], side_by_side, preferred_element_type=F32
            ).astype(BF16)

        def operator_part(q):
            def stacked(g):
                row = (4 * q + g) * TILE
                return jnp.concatenate(
                    [inner[row : row + TILE, w * blk : (w + 1) * blk] for w in range(chan)], axis=0
                )

            even = jnp.dot(
                spread[...], jnp.concatenate([stacked(0), stacked(2)], axis=1),
                preferred_element_type=F32,
            )
            odd = jnp.dot(
                flipped[...], jnp.concatenate([stacked(1), stacked(3)], axis=1),
                preferred_element_type=F32,
            )
            low = jnp.where(low_rows, even, odd)
            high = jnp.where(low_rows, odd, even)
            for s in range(phys):
                for m in range(chan // 2):
                    row = s * chan * group + m * 2 * group
                    for k, tile in enumerate((low, high)):
                        tile = tile[row : row + 2 * group]
                        if k:
                            tile = pltpu.roll(tile, group, 0)
                        tile = jnp.concatenate([tile[:, :blk], tile[:, blk:]], axis=0).astype(BF16)
                        at = (2 * m + k) * blk + q * TILE
                        mixed[at : at + TILE, s * blk : (s + 1) * blk] = tile

        rights = [functools.partial(right_part, h, w) for h in range(2) for w in range(0, chan, 2)]
        return rights, [functools.partial(operator_part, q) for q in range(wide // (4 * TILE))]

    def close(n, j, vector, mixed, value):
        held = {"along": [zero] * STEPS, "whole": zero, "norm": zero}

        def left_part():
            rows = jnp.concatenate([left_in[n, u] for u in range(chan)], axis=1)
            result = jnp.dot(rows, mixed[...], preferred_element_type=F32)
            for s in range(phys):
                value[0, pl.ds(s, blk, stride=phys), :] = result[:, s * blk : (s + 1) * blk]

        def image_part(r):
            image = value[0, r : r + chunk] + column[n, r : r + chunk] * vector[n, r : r + chunk].astype(F32)
            value[0, r : r + chunk] = image
            held["whole"] = held["whole"] + sum8(image * image)
            held["along"] = [
                a + sum8(basis[n, i, r : r + chunk] * image) for i, a in enumerate(held["along"])
            ]

        def number_part():
            along, whole = [spread_sum(a) for a in held["along"]], spread_sum(held["whole"])
            shares = [share_of(a, norms[n, i : i + 1]) for i, a in enumerate(along)]
            square = whole
            for a, c in zip(along, shares):
                square = square - a * c
            held["shares"] = shares
            held["length"], held["inverse"] = length_of(square, whole)

        def probe_part(r):
            probe = value[here_zero, r : r + chunk]
            for i, c in enumerate(held["shares"]):
                probe = probe - c * basis[n + here_zero, i, r : r + chunk]
            probe = probe * held["inverse"]
            vector[n, r : r + chunk] = probe.astype(BF16)
            basis[n, j + 1, r : r + chunk] = probe
            held["norm"] = held["norm"] + sum8(probe * probe)

        def record_part():
            norm = spread_sum(held["norm"])
            norms[n] = jnp.where(line8 == j + 1, norm, norms[n])
            row = jnp.zeros((1, blk), F32)
            for i, number in enumerate([*held["shares"], held["length"], norm]):
                row = jnp.where(lane == 8 * j + i, number, row)
            part[...] = jnp.where((line8 == n) & (lane8 // 8 == j), row, part[...])

        images = [functools.partial(image_part, r) for r in range(0, wide, chunk)]
        probes = [functools.partial(probe_part, r) for r in range(0, wide, chunk)]
        return left_part, images, number_part, probes, record_part

    def run(parts):
        for one in parts:
            one()

    def beside(closing, contracting):
        left_part, images, number_part, probes, record_part = closing
        rights, operators = contracting
        run(rights[:4])
        left_part()
        run(rights[4:8])
        for k, one in enumerate(images):
            one()
            run(rights[8 + k : 9 + k])
        number_part()
        operators[0]()
        operators[1]()
        for k, one in enumerate(probes):
            one()
            if k % 2:
                run(operators[2 + k // 2 : 3 + k // 2])
        run(operators[6:])
        record_part()

    def before(closing, contracting):
        left_part, images, number_part, probes, record_part = closing
        rights, operators = contracting
        left_part()
        run(images)
        number_part()
        run(probes[:4])
        for k, one in enumerate(probes[4:]):
            run(rights[2 * k : 2 * k + 2])
            one()
        run(rights[8:])
        record_part()
        run(operators)

    def alone(closing):
        left_part, images, number_part, probes, record_part = closing
        left_part()
        run(images)
        number_part()
        run(probes)
        record_part()

    for n in range(slots):
        open_slot(n)
    for parts in contract(0, vector_a, inner_a, mixed_a):
        run(parts)

    decay_all[me] = decay[...]
    energy_all[me] = energy[...]
    for k in range(1, regions):
        for copy in prefix_copies(k, lax.rem(me + regions - k, regions)):
            copy.wait()
    offsets = jnp.zeros((slots, blk), F32)
    for p in range(regions - 1):
        offsets = jnp.where(p < me, decay_all[p] * offsets + energy_all[p], offsets)
    for n in range(slots):
        turned = jnp.broadcast_to(offsets[n : n + 1], (blk, blk)).T
        for s in range(phys):
            column[n, pl.ds(s, blk, stride=phys), :] = turned

    @pl.when(jnp.logical_not(crossing))
    def _():
        for n in range(slots):
            own_copy(n).wait()

    def both(i, carry):
        n, j = i // STEPS * 2, i % STEPS
        after = (i + 1) % (slots // 2 * STEPS)
        beside(close(n, j, vector_a, mixed_a, value_a), contract(n + 1, vector_b, inner_b, mixed_b))
        beside(
            close(n + 1, j, vector_b, mixed_b, value_b),
            contract(after // STEPS * 2, vector_a, inner_a, mixed_a),
        )
        return carry

    lax.fori_loop(0, rounds, both, 0)

    def single(n, carry):
        own_copy(n).wait()
        chain = vector_b, inner_b, mixed_b
        before(close(n, 0, vector_b, mixed_a, value_b), contract(n, *chain))
        before(close(n, 1, vector_b, mixed_b, value_b), contract(n, *chain))

        def last():
            return close(n, STEPS - 1, vector_b, mixed_b, value_b)

        @pl.when(n < slots - 1)
        def _():
            beside(last(), contract(n + 1, vector_a, inner_a, mixed_a))

        @pl.when(n == slots - 1)
        def _():
            alone(last())

        return carry

    lax.fori_loop(0, singles, single, 0)

    gathered[mine] = part[...]

    def copy_of(k, slot):
        return pltpu.make_async_remote_copy(
            src_ref=part, dst_ref=gathered.at[slot],
            send_sem=sum_send.at[k - 1], recv_sem=sum_recv.at[k - 1],
            device_id={"sector": lax.rem(mine + k, sectors)}, device_id_type=MESH,
        )

    for k in range(1, sectors):
        copy_of(k, mine).start()
    for k in range(1, sectors):
        copy_of(k, lax.rem(mine + sectors - k, sectors)).wait()
    many = sectors * 8
    table = gathered[...].reshape(many, blk).T
    images = [[table[8 * j + i : 8 * j + i + 1] for i in range(STEPS)] + [None] for j in range(STEPS)]
    gram = {0: table[8 * STEPS : 8 * STEPS + 1]}
    for j in range(STEPS):
        length = table[8 * j + STEPS : 8 * j + STEPS + 1]
        images[j] = [c if i <= j else None for i, c in enumerate(images[j])]
        images[j][j + 1] = length
        gram[j + 1] = table[8 * j + STEPS + 1 : 8 * j + STEPS + 2]

    def inner(x, y):
        total = jnp.zeros((1, many), F32)
        for i, (xi, yi) in enumerate(zip(x, y)):
            if xi is not None and yi is not None:
                total = total + xi * yi * gram[i]
        return jnp.broadcast_to(jnp.sum(total, axis=1, keepdims=True), (1, many))

    def mix(p, x, q, y):
        def one(a, b):
            if a is None:
                return None if b is None else q * b
            return p * a if b is None else p * a + q * b

        return [one(a, b) for a, b in zip(x, y)]

    unit = jnp.ones((1, many), F32)
    inverse = lax.rsqrt(inner([unit] + [None] * STEPS, [unit] + [None] * STEPS) + EPS)
    current = [inverse * unit, None, None, None]
    applied = [inverse * a if a is not None else None for a in images[0]]
    for _ in range(DAV):
        quotient = inner(current, applied)
        residual = mix(1.0, applied, -quotient, current)
        resid_sq = inner(residual, residual)
        factor = lax.rsqrt(resid_sq + EPS)
        search = [factor * a if a is not None else None for a in residual]
        moved = [None] * (STEPS + 1)
        for a, line in zip(search, images):
            if a is not None:
                moved = mix(1.0, moved, a, line)
        curvature = inner(search, moved)
        cos_part, sin_part = half_rotation(-2.0 * resid_sq * factor, curvature - quotient)
        current = mix(cos_part, current, sin_part, search)
        applied = mix(cos_part, applied, sin_part, moved)
    energy_out[...] = jnp.broadcast_to(inner(current, applied)[:, :1], (8, blk))
    scale = math.sqrt(slots * sectors * blk * phys * blk)

    for n in range(slots):
        here = lax.broadcasted_iota(jnp.int32, (1, many), 1) == mine * 8 + n
        factors = [
            jnp.broadcast_to(jnp.sum(jnp.where(here, scale * c, 0.0), axis=1, keepdims=True), (1, blk))
            for c in current[:STEPS]
        ]
        for r in range(0, wide, chunk):
            state = jnp.zeros((chunk, blk), F32)
            for i, c in enumerate(factors):
                state = state + c * basis[n, i, r : r + chunk]
            state_out[n, r : r + chunk] = state.astype(BF16)

    @pl.when(me < regions - 1)
    def _():
        for n in range(slots):
            left_copy(n).wait_send()


def finish(state, energy, out, density, energy_out, rows_buf, density_buf, sems):
    slots, wide, blk = state.shape
    phys = wide // blk
    copies = [pltpu.make_async_copy(state, out, sems.at[slots])]
    copies[0].start()
    for n in range(slots):
        rows_buf[n] = state[n].astype(F32)
        total = jnp.zeros((blk, blk), F32)
        for s in range(phys):
            rows = rows_buf[n, pl.ds(s, blk, stride=phys), :].astype(BF16)
            total = total + lax.dot_general(
                rows, rows, (((1,), (1,)), ((), ())), preferred_element_type=F32
            )
        density_buf[n] = total / (phys * blk)
        copies.append(pltpu.make_async_copy(density_buf.at[n], density.at[n], sems.at[n]))
        copies[-1].start()
    energy_out[0] = energy[0, 0]
    for copy in copies:
        copy.wait()


def body(regions, sectors, start_state, left_env, right_env, mpo_tensor, decay, energy_terms, live_count):
    _, slots, blk, phys, _ = start_state.shape
    chan = left_env.shape[2]
    wide = phys * blk
    side = chan * TILE
    vmem = pl.BlockSpec(memory_space=pltpu.VMEM)
    hbm = pl.BlockSpec(memory_space=pltpu.HBM)
    smem = pl.BlockSpec(memory_space=pltpu.SMEM)
    dma = pltpu.SemaphoreType.DMA
    twice = lambda *spec: [pltpu.VMEM(*spec)] * 2
    outs = pl.pallas_call(
        functools.partial(kernel, regions, sectors),
        out_shape=(
            jax.ShapeDtypeStruct((slots, wide, blk), BF16),
            jax.ShapeDtypeStruct((8, blk), F32),
        ),
        in_specs=[hbm, hbm, hbm, vmem, vmem, vmem, vmem],
        out_specs=(vmem, vmem),
        scratch_shapes=[
            pltpu.VMEM((slots, wide, blk), BF16),
            pltpu.VMEM((slots, chan, blk, blk), BF16),
            pltpu.VMEM((slots, chan, blk, blk), BF16),
            pltpu.VMEM((chan * phys * phys, chan), F32),
            *twice((side, side), BF16),
            pltpu.VMEM((slots, wide, blk), F32),
            *twice((slots, wide, blk), BF16),
            *twice((wide, chan * blk), BF16),
            *twice((chan * blk, wide), BF16),
            *twice((1, wide, blk), F32),
            pltpu.VMEM((slots, STEPS + 1, wide, blk), F32),
            pltpu.VMEM((slots, 8, blk), F32),
            pltpu.VMEM((regions, slots, blk), F32),
            pltpu.VMEM((regions, slots, blk), F32),
            pltpu.VMEM((8, blk), F32),
            pltpu.VMEM((sectors, 8, blk), F32),
            dma((slots,)), dma((slots,)), dma((slots,)), dma((slots,)),
            dma((2, regions)), dma((2, regions)),
            dma((sectors,)), dma((sectors,)),
        ],
        compiler_params=pltpu.CompilerParams(
            collective_id=0, has_side_effects=True, vmem_limit_bytes=60 * 2**20
        ),
    )(
        start_state.reshape(slots, wide, blk), left_env[0], right_env[0],
        mpo_tensor.reshape(chan * phys * phys, chan),
        decay[0], energy_terms[0], live_count,
    )
    state_out, density, energy = pl.pallas_call(
        finish,
        out_shape=(
            jax.ShapeDtypeStruct((slots, wide, blk), BF16),
            jax.ShapeDtypeStruct((slots, blk, blk), F32),
            jax.ShapeDtypeStruct((1,), F32),
        ),
        in_specs=[vmem, vmem],
        out_specs=(hbm, hbm, smem),
        scratch_shapes=[
            pltpu.VMEM((slots, wide, blk), F32),
            pltpu.VMEM((slots, blk, blk), F32),
            dma((slots + 1,)),
        ],
    )(*outs)
    return (
        state_out.reshape(start_state.shape),
        density.reshape(1, slots, blk, blk),
        energy,
    )


def solution(mesh):
    in_specs = (
        P("region", "sector", None, None, None),
        P("region", "sector", None, None, None),
        P("region", "sector", None, None, None),
        P(),
        P("region", "sector", None),
        P("region", "sector", None),
        P("region", "sector"),
    )
    out_specs = (
        P("region", "sector", None, None, None),
        P("region", "sector", None, None),
        P("region"),
    )
    step = functools.partial(body, mesh.shape["region"], mesh.shape["sector"])
    return jax.shard_map(step, mesh=mesh, in_specs=in_specs, out_specs=out_specs, check_vma=False)
```

```python
import functools
import math

import jax
import jax.numpy as jnp
from jax import lax
from jax.experimental import pallas as pl
from jax.experimental.pallas import tpu as pltpu
from jax.sharding import PartitionSpec as P

DAV = 2
EPS = 1e-06
MESH = pl.DeviceIdType.MESH
F32 = jnp.float32
BF16 = jnp.bfloat16
STEPS = DAV + 1
TILE = 16


def half_rotation(y, x):
    top = jnp.maximum(jnp.abs(x), jnp.abs(y))
    safe = jnp.where(top > 0, top, 1.0)
    xn, yn = x / safe, y / safe
    h = jnp.sqrt(xn * xn + yn * yn)
    h = jnp.where(top > 0, h, 1.0)
    big = jnp.sqrt(0.5 * (h + jnp.abs(xn)) / h)
    small = jnp.abs(yn) / (2.0 * h * big)
    big = jnp.where(top > 0, big, 1.0)
    small = jnp.where(top > 0, small, 0.0)
    cos_part = jnp.where(x >= 0, big, small)
    sin_size = jnp.where(x >= 0, small, big)
    return cos_part, jnp.where(y > 0, sin_size, -sin_size)


def kernel(
    regions, sectors, start, left, right, operator, decay, energy, live,
    state_out, energy_out,
    operator_in, live_in, state_buf, energy_buf, start_in, left_in, right_in, lines, spread, flipped, column,
    vector_a, vector_b, inner_a, inner_b, mixed_a, mixed_b, value_a, value_b,
    basis, norms, decay_all, energy_all, part, gathered,
    left_send, left_recv, right_sem, start_sem, small_sem, out_sem, pre_send, pre_recv, sum_send, sum_recv,
):
    slots, chan, blk, _ = left.shape
    wide = start.shape[1]
    phys = wide // blk
    me, mine = lax.axis_index("region"), lax.axis_index("sector")
    group = TILE // phys
    side = chan * TILE
    here_zero = me // regions
    crossing = (me > 0) & (me % 2 == 0)
    rounds = jnp.where(crossing, 0, slots // 2 * STEPS)
    singles = jnp.where(crossing, slots, 0)
    barrier = pltpu.get_barrier_semaphore()
    for k in range(1, regions):
        pl.semaphore_signal(
            barrier, 1, device_id={"region": lax.rem(me + k, regions)}, device_id_type=MESH
        )
    for k in range(1, sectors):
        pl.semaphore_signal(
            barrier, 1, device_id={"sector": lax.rem(mine + k, sectors)}, device_id_type=MESH
        )
    small = [
        pltpu.make_async_copy(src, dst, small_sem.at[i])
        for i, (src, dst) in enumerate((
            (operator, operator_in), (live, live_in), (decay, decay_all.at[me]), (energy, energy_all.at[me]),
        ))
    ]
    for copy in small:
        copy.start()
    for n in range(slots):
        pltpu.make_async_copy(right.at[n], right_in.at[n], right_sem.at[n]).start()
        pltpu.make_async_copy(start.at[n], start_in.at[n], start_sem.at[n]).start()
    pl.semaphore_wait(barrier, regions + sectors - 2)

    def left_copy(n):
        return pltpu.make_async_remote_copy(
            src_ref=left.at[n], dst_ref=left_in.at[n],
            send_sem=left_send.at[n], recv_sem=left_recv.at[n],
            device_id={"region": lax.rem(me + 1, regions)}, device_id_type=MESH,
        )

    def own_copy(n):
        return pltpu.make_async_copy(left.at[n], left_in.at[n], left_recv.at[n])

    def prefix_copies(k, slot):
        to = {"region": lax.rem(me + k, regions)}
        return [
            pltpu.make_async_remote_copy(
                src_ref=src, dst_ref=dst.at[slot],
                send_sem=pre_send.at[i, k - 1], recv_sem=pre_recv.at[i, k - 1],
                device_id=to, device_id_type=MESH,
            )
            for i, (src, dst) in enumerate(((decay, decay_all), (energy, energy_all)))
        ]

    for k in range(1, regions):

        @pl.when(me + k < regions)
        def _():
            for copy in prefix_copies(k, me):
                copy.start()

    @pl.when(me < regions - 1)
    def _():
        for n in range(slots):
            left_copy(n).start()

    @pl.when(me == 0)
    def _():
        for n in range(slots):
            own_copy(n).start()

    for copy in small:
        copy.wait()
    live_slots = live_in[...]
    part[...] = jnp.zeros_like(part)

    lines[...] = operator_in[...].astype(F32)

    def where_one(test):
        return jnp.where(test, 1.0, 0.0).astype(BF16)

    def grid_of(shape):
        return [lax.broadcasted_iota(jnp.int32, shape, i) for i in range(2)]

    def spread_operator(out, swap):
        r, c = grid_of((side, chan * phys))
        u = (r // group) % chan
        if swap:
            u = u + 1 - 2 * (u % 2)
        pick_row = where_one((c // phys == u) & (c % phys == r // (chan * group)))
        r, c = grid_of((chan, side))
        total = jnp.zeros((side, side), F32)
        for t in range(phys):
            tall = jnp.dot(
                pick_row,
                lines[pl.ds(t, chan * phys, stride=phys), :].astype(BF16),
                preferred_element_type=F32,
            ).astype(BF16)
            pick_column = where_one((c // TILE == r) & (c % phys == t))
            total = total + jnp.dot(tall, pick_column, preferred_element_type=F32)
        r, c = grid_of((side, side))
        out[...] = jnp.where(r % group == (c // phys) % group, total, 0.0).astype(BF16)

    spread_operator(spread, False)
    spread_operator(flipped, True)

    def sum8(value):
        return jnp.sum(value.reshape(-1, 8, value.shape[-1]), axis=0)

    def spread_sum(total):
        return jnp.broadcast_to(jnp.sum(total, keepdims=True).reshape(1, 1), (1, blk))

    def length_of(square, whole):
        square = jnp.maximum(square, 1e-10 * whole)
        inverse = jnp.where(square > 0, lax.rsqrt(jnp.where(square > 0, square, 1.0)), 0.0)
        return square * inverse, inverse

    def share_of(value, norm):
        return jnp.where(norm > 0, value / jnp.where(norm > 0, norm, 1.0), 0.0)

    zero = jnp.zeros((8, blk), F32)
    lane = lax.broadcasted_iota(jnp.int32, (1, blk), 1)
    lane8 = lax.broadcasted_iota(jnp.int32, (8, blk), 1)
    line8 = lax.broadcasted_iota(jnp.int32, (8, blk), 0)
    chunk = 64

    def open_slot(n):
        pltpu.make_async_copy(right.at[n], right_in.at[n], right_sem.at[n]).wait()
        pltpu.make_async_copy(start.at[n], start_in.at[n], start_sem.at[n]).wait()
        alive = jnp.broadcast_to(jnp.where(n < live_slots, 1.0, 0.0), (1, blk)).astype(F32)
        total = zero
        for r in range(0, wide, chunk):
            first = start_in[n, r : r + chunk].astype(F32) * alive
            basis[n, 0, r : r + chunk] = first
            vector_a[n, r : r + chunk] = first.astype(BF16)
            vector_b[n, r : r + chunk] = first.astype(BF16)
            total = total + sum8(first * first)
            for i in range(1, STEPS):
                basis[n, i, r : r + chunk] = jnp.zeros((chunk, blk), F32)
        total = spread_sum(total)
        norms[n] = jnp.where(line8 == 0, total, 0.0)
        part[...] = jnp.where((line8 == n) & (lane8 == 8 * STEPS), total, part[...])

    low_rows = lax.broadcasted_iota(jnp.int32, (side, 2 * blk), 0) % (2 * group) < group

    def contract(n, vector, inner, mixed):
        half = wide // 2

        def right_part(h, w):
            side_by_side = jnp.concatenate([right_in[n, w], right_in[n, w + 1]], axis=1)
            inner[h * half : (h + 1) * half, w * blk : (w + 2) * blk] = jnp.dot(
                vector[n, h * half : (h + 1) * half], side_by_side, preferred_element_type=F32
            ).astype(BF16)

        def operator_part(q):
            def stacked(g):
                row = (4 * q + g) * TILE
                return jnp.concatenate(
                    [inner[row : row + TILE, w * blk : (w + 1) * blk] for w in range(chan)], axis=0
                )

            even = jnp.dot(
                spread[...], jnp.concatenate([stacked(0), stacked(2)], axis=1),
                preferred_element_type=F32,
            )
            odd = jnp.dot(
                flipped[...], jnp.concatenate([stacked(1), stacked(3)], axis=1),
                preferred_element_type=F32,
            )
            low = jnp.where(low_rows, even, odd)
            high = jnp.where(low_rows, odd, even)
            for s in range(phys):
                for m in range(chan // 2):
                    row = s * chan * group + m * 2 * group
                    for k, tile in enumerate((low, high)):
                        tile = tile[row : row + 2 * group]
                        if k:
                            tile = pltpu.roll(tile, group, 0)
                        tile = jnp.concatenate([tile[:, :blk], tile[:, blk:]], axis=0).astype(BF16)
                        at = (2 * m + k) * blk + q * TILE
                        mixed[at : at + TILE, s * blk : (s + 1) * blk] = tile

        rights = [functools.partial(right_part, h, w) for h in range(2) for w in range(0, chan, 2)]
        return rights, [functools.partial(operator_part, q) for q in range(wide // (4 * TILE))]

    def close(n, j, vector, mixed, value, final=False):
        held = {"along": [zero] * STEPS, "whole": zero, "norm": zero}

        def left_part():
            rows = jnp.concatenate([left_in[n, u] for u in range(chan)], axis=1)
            result = jnp.dot(rows, mixed[...], preferred_element_type=F32)
            for s in range(phys):
                value[0, pl.ds(s, blk, stride=phys), :] = result[:, s * blk : (s + 1) * blk]

        def image_part(r):
            image = value[0, r : r + chunk] + column[n, r : r + chunk] * vector[n, r : r + chunk].astype(F32)
            value[0, r : r + chunk] = image
            held["whole"] = held["whole"] + sum8(image * image)
            held["along"] = [
                a + sum8(basis[n, i, r : r + chunk] * image) for i, a in enumerate(held["along"])
            ]

        def number_part():
            along, whole = [spread_sum(a) for a in held["along"]], spread_sum(held["whole"])
            shares = [share_of(a, norms[n, i : i + 1]) for i, a in enumerate(along)]
            square = whole
            for a, c in zip(along, shares):
                square = square - a * c
            held["shares"] = shares
            held["length"], held["inverse"] = length_of(square, whole)

        def probe_part(r):
            probe = value[here_zero, r : r + chunk]
            for i, c in enumerate(held["shares"]):
                probe = probe - c * basis[n + here_zero, i, r : r + chunk]
            probe = probe * held["inverse"]
            vector[n, r : r + chunk] = probe.astype(BF16)
            basis[n, j + 1, r : r + chunk] = probe
            held["norm"] = held["norm"] + sum8(probe * probe)

        def record_part():
            numbers = [*held["shares"]]
            if not final:
                norm = spread_sum(held["norm"])
                norms[n] = jnp.where(line8 == j + 1, norm, norms[n])
                numbers += [held["length"], norm]
            row = jnp.zeros((1, blk), F32)
            for i, number in enumerate(numbers):
                row = jnp.where(lane == 8 * j + i, number, row)
            part[...] = jnp.where((line8 == n) & (lane8 // 8 == j), row, part[...])

        images = [functools.partial(image_part, r) for r in range(0, wide, chunk)]
        probes = [] if final else [functools.partial(probe_part, r) for r in range(0, wide, chunk)]
        return left_part, images, number_part, probes, record_part

    def run(parts):
        for one in parts:
            one()

    def beside(closing, contracting):
        left_part, images, number_part, probes, record_part = closing
        rights, operators = contracting
        run(rights[:4])
        left_part()
        run(rights[4:8])
        for k, one in enumerate(images):
            one()
            run(rights[8 + k : 9 + k])
        number_part()
        operators[0]()
        operators[1]()
        if not probes:
            record_part()
        for k, one in enumerate(probes):
            one()
            if k % 2:
                run(operators[2 + k // 2 : 3 + k // 2])
        run(operators[6 if probes else 2 :])
        if probes:
            record_part()

    def before(closing, contracting):
        left_part, images, number_part, probes, record_part = closing
        rights, operators = contracting
        left_part()
        run(images)
        number_part()
        run(probes[:4])
        for k, one in enumerate(probes[4:]):
            run(rights[2 * k : 2 * k + 2])
            one()
        run(rights[8:])
        record_part()
        run(operators)

    def alone(closing):
        left_part, images, number_part, probes, record_part = closing
        left_part()
        run(images)
        number_part()
        run(probes)
        record_part()

    for n in range(slots):
        open_slot(n)
    for parts in contract(0, vector_a, inner_a, mixed_a):
        run(parts)

    for k in range(1, regions):

        @pl.when(me + k < regions)
        def _():
            for copy in prefix_copies(k, me):
                copy.wait_send()

        @pl.when(me >= k)
        def _():
            for copy in prefix_copies(k, lax.rem(me + regions - k, regions)):
                copy.wait_recv()

    offsets = jnp.zeros((slots, blk), F32)
    for p in range(regions - 1):
        offsets = jnp.where(p < me, decay_all[p] * offsets + energy_all[p], offsets)
    for n in range(slots):
        turned = jnp.broadcast_to(offsets[n : n + 1], (blk, blk)).T
        for s in range(phys):
            column[n, pl.ds(s, blk, stride=phys), :] = turned

    @pl.when(jnp.logical_not(crossing))
    def _():
        for n in range(slots):
            own_copy(n).wait()

    def both(i, carry):
        n, j = i // STEPS * 2, i % STEPS
        after = (i + 1) % (slots // 2 * STEPS)
        beside(close(n, j, vector_a, mixed_a, value_a), contract(n + 1, vector_b, inner_b, mixed_b))
        beside(
            close(n + 1, j, vector_b, mixed_b, value_b),
            contract(after // STEPS * 2, vector_a, inner_a, mixed_a),
        )
        return carry

    lax.fori_loop(0, rounds, both, 0)

    def single(n, carry):
        own_copy(n).wait()
        chain = vector_b, inner_b, mixed_b
        before(close(n, 0, vector_b, mixed_a, value_b), contract(n, *chain))
        before(close(n, 1, vector_b, mixed_b, value_b), contract(n, *chain))

        def last():
            return close(n, STEPS - 1, vector_b, mixed_b, value_b, final=True)

        @pl.when(n < slots - 1)
        def _():
            beside(last(), contract(n + 1, vector_a, inner_a, mixed_a))

        @pl.when(n == slots - 1)
        def _():
            alone(last())

        return carry

    lax.fori_loop(0, singles, single, 0)

    gathered[mine] = part[...]

    def copy_of(k, slot):
        return pltpu.make_async_remote_copy(
            src_ref=part, dst_ref=gathered.at[slot],
            send_sem=sum_send.at[k - 1], recv_sem=sum_recv.at[k - 1],
            device_id={"sector": lax.rem(mine + k, sectors)}, device_id_type=MESH,
        )

    for k in sorted(range(1, sectors), key=lambda k: abs(2 * k - sectors)):
        copy_of(k, mine).start()
    for k in range(1, sectors):
        copy_of(k, lax.rem(mine + sectors - k, sectors)).wait()
    many = sectors * 8
    table = gathered[...].reshape(many, blk).T
    images = [[table[8 * j + i : 8 * j + i + 1] for i in range(STEPS)] + [None] for j in range(STEPS)]
    gram = {0: table[8 * STEPS : 8 * STEPS + 1]}
    for j in range(STEPS):
        length = table[8 * j + STEPS : 8 * j + STEPS + 1]
        images[j] = [c if i <= j else None for i, c in enumerate(images[j])]
        images[j][j + 1] = length
        gram[j + 1] = table[8 * j + STEPS + 1 : 8 * j + STEPS + 2]

    def inner(x, y):
        total = jnp.zeros((1, many), F32)
        for i, (xi, yi) in enumerate(zip(x, y)):
            if xi is not None and yi is not None:
                total = total + xi * yi * gram[i]
        return jnp.broadcast_to(jnp.sum(total, axis=1, keepdims=True), (1, many))

    def mix(p, x, q, y):
        def one(a, b):
            if a is None:
                return None if b is None else q * b
            return p * a if b is None else p * a + q * b

        return [one(a, b) for a, b in zip(x, y)]

    unit = jnp.ones((1, many), F32)
    inverse = lax.rsqrt(inner([unit] + [None] * STEPS, [unit] + [None] * STEPS) + EPS)
    current = [inverse * unit, None, None, None]
    applied = [inverse * a if a is not None else None for a in images[0]]
    for _ in range(DAV):
        quotient = inner(current, applied)
        residual = mix(1.0, applied, -quotient, current)
        resid_sq = inner(residual, residual)
        factor = lax.rsqrt(resid_sq + EPS)
        search = [factor * a if a is not None else None for a in residual]
        moved = [None] * (STEPS + 1)
        for a, line in zip(search, images):
            if a is not None:
                moved = mix(1.0, moved, a, line)
        curvature = inner(search, moved)
        cos_part, sin_part = half_rotation(-2.0 * resid_sq * factor, curvature - quotient)
        current = mix(cos_part, current, sin_part, search)
        applied = mix(cos_part, applied, sin_part, moved)
    energy_buf[...] = jnp.broadcast_to(inner(current, applied)[:, :1], (8, blk))
    scale = math.sqrt(slots * sectors * blk * phys * blk)

    copies = [pltpu.make_async_copy(energy_buf, energy_out, out_sem.at[slots])]
    copies[0].start()
    for n in range(slots):
        here = lax.broadcasted_iota(jnp.int32, (1, many), 1) == mine * 8 + n
        factors = [
            jnp.broadcast_to(jnp.sum(jnp.where(here, scale * c, 0.0), axis=1, keepdims=True), (1, blk))
            for c in current[:STEPS]
        ]
        for r in range(0, wide, chunk):
            state = jnp.zeros((chunk, blk), F32)
            for i, c in enumerate(factors):
                state = state + c * basis[n, i, r : r + chunk]
            state_buf[n, r : r + chunk] = state.astype(BF16)
        copies.append(pltpu.make_async_copy(state_buf.at[n], state_out.at[n], out_sem.at[n]))
        copies[-1].start()
    for copy in copies:
        copy.wait()

    @pl.when(me < regions - 1)
    def _():
        for n in range(slots):
            left_copy(n).wait_send()


def finish(state, energy, out, density, energy_out, rows_buf, density_buf, energy_buf, sems):
    slots, wide, blk = state.shape
    phys = wide // blk
    energy_buf[0] = energy[0, 0]
    copies = [
        pltpu.make_async_copy(state, out, sems.at[slots]),
        pltpu.make_async_copy(energy_buf, energy_out, sems.at[slots + 1]),
    ]
    for copy in copies:
        copy.start()
    for n in range(slots):
        rows_buf[n] = state[n].astype(F32)
        total = jnp.zeros((blk, blk), F32)
        for s in range(phys):
            rows = rows_buf[n, pl.ds(s, blk, stride=phys), :].astype(BF16)
            total = total + lax.dot_general(
                rows, rows, (((1,), (1,)), ((), ())), preferred_element_type=F32
            )
        density_buf[n] = total / (phys * blk)
        copies.append(pltpu.make_async_copy(density_buf.at[n], density.at[n], sems.at[n]))
        copies[-1].start()
    for copy in copies:
        copy.wait()


def body(regions, sectors, start_state, left_env, right_env, mpo_tensor, decay, energy_terms, live_count):
    _, slots, blk, phys, _ = start_state.shape
    chan = left_env.shape[2]
    wide = phys * blk
    side = chan * TILE
    vmem = pl.BlockSpec(memory_space=pltpu.VMEM)
    hbm = pl.BlockSpec(memory_space=pltpu.HBM)
    dma = pltpu.SemaphoreType.DMA
    twice = lambda *spec: [pltpu.VMEM(*spec)] * 2
    outs = pl.pallas_call(
        functools.partial(kernel, regions, sectors),
        out_shape=(
            jax.ShapeDtypeStruct((slots, wide, blk), BF16),
            jax.ShapeDtypeStruct((8, blk), F32),
        ),
        in_specs=[hbm] * 7,
        out_specs=(hbm, hbm),
        scratch_shapes=[
            pltpu.VMEM((chan * phys * phys, chan), BF16),
            pltpu.VMEM((1, 1), jnp.int32),
            pltpu.VMEM((slots, wide, blk), BF16),
            pltpu.VMEM((8, blk), F32),
            pltpu.VMEM((slots, wide, blk), BF16),
            pltpu.VMEM((slots, chan, blk, blk), BF16),
            pltpu.VMEM((slots, chan, blk, blk), BF16),
            pltpu.VMEM((chan * phys * phys, chan), F32),
            *twice((side, side), BF16),
            pltpu.VMEM((slots, wide, blk), F32),
            *twice((slots, wide, blk), BF16),
            *twice((wide, chan * blk), BF16),
            *twice((chan * blk, wide), BF16),
            *twice((1, wide, blk), F32),
            pltpu.VMEM((slots, STEPS + 1, wide, blk), F32),
            pltpu.VMEM((slots, 8, blk), F32),
            pltpu.VMEM((regions, slots, blk), F32),
            pltpu.VMEM((regions, slots, blk), F32),
            pltpu.VMEM((8, blk), F32),
            pltpu.VMEM((sectors, 8, blk), F32),
            dma((slots,)), dma((slots,)), dma((slots,)), dma((slots,)), dma((4,)), dma((slots + 1,)),
            dma((2, regions)), dma((2, regions)),
            dma((sectors,)), dma((sectors,)),
        ],
        compiler_params=pltpu.CompilerParams(
            collective_id=0, has_side_effects=True, vmem_limit_bytes=60 * 2**20
        ),
    )(
        start_state.reshape(slots, wide, blk), left_env[0], right_env[0],
        mpo_tensor.reshape(chan * phys * phys, chan),
        decay[0], energy_terms[0], live_count,
    )
    state_out, density, energy = pl.pallas_call(
        finish,
        out_shape=(
            jax.ShapeDtypeStruct((slots, wide, blk), BF16),
            jax.ShapeDtypeStruct((slots, blk, blk), F32),
            jax.ShapeDtypeStruct((1,), F32),
        ),
        in_specs=[vmem, vmem],
        out_specs=(hbm, hbm, hbm),
        scratch_shapes=[
            pltpu.VMEM((slots, wide, blk), F32),
            pltpu.VMEM((slots, blk, blk), F32),
            pltpu.SMEM((1,), F32),
            dma((slots + 2,)),
        ],
    )(*outs)
    return (
        state_out.reshape(start_state.shape),
        density.reshape(1, slots, blk, blk),
        energy,
    )


def solution(mesh):
    in_specs = (
        P("region", "sector", None, None, None),
        P("region", "sector", None, None, None),
        P("region", "sector", None, None, None),
        P(),
        P("region", "sector", None),
        P("region", "sector", None),
        P("region", "sector"),
    )
    out_specs = (
        P("region", "sector", None, None, None),
        P("region", "sector", None, None),
        P("region"),
    )
    step = functools.partial(body, mesh.shape["region"], mesh.shape["sector"])
    return jax.shard_map(step, mesh=mesh, in_specs=in_specs, out_specs=out_specs, check_vma=False)
```

```python
import functools
import math

import jax
import jax.numpy as jnp
from jax import lax
from jax.experimental import pallas as pl
from jax.experimental.pallas import tpu as pltpu
from jax.sharding import PartitionSpec as P

DAV = 2
EPS = 1e-06
MESH = pl.DeviceIdType.MESH
F32 = jnp.float32
BF16 = jnp.bfloat16
STEPS = DAV + 1
TILE = 16


def half_rotation(y, x):
    top = jnp.maximum(jnp.abs(x), jnp.abs(y))
    safe = jnp.where(top > 0, top, 1.0)
    xn, yn = x / safe, y / safe
    h = jnp.sqrt(xn * xn + yn * yn)
    h = jnp.where(top > 0, h, 1.0)
    big = jnp.sqrt(0.5 * (h + jnp.abs(xn)) / h)
    small = jnp.abs(yn) / (2.0 * h * big)
    big = jnp.where(top > 0, big, 1.0)
    small = jnp.where(top > 0, small, 0.0)
    cos_part = jnp.where(x >= 0, big, small)
    sin_size = jnp.where(x >= 0, small, big)
    return cos_part, jnp.where(y > 0, sin_size, -sin_size)


def kernel(
    regions, sectors, start, left, right, operator, decay, energy, live,
    state_out, energy_out,
    operator_in, live_in, state_buf, energy_buf, start_in, left_in, right_in, lines, spread, flipped, column,
    vector_a, vector_b, inner_a, inner_b, mixed_a, mixed_b, value_a, value_b,
    basis, norms, decay_all, energy_all, part, gathered,
    left_send, left_recv, right_sem, start_sem, small_sem, out_sem, pre_send, pre_recv, sum_send, sum_recv,
):
    slots, chan, blk, _ = left.shape
    wide = start.shape[1]
    phys = wide // blk
    me, mine = lax.axis_index("region"), lax.axis_index("sector")
    group = TILE // phys
    side = chan * TILE
    here_zero = me // regions
    crossing = (me > 0) & (me % 2 == 0)
    rounds = jnp.where(crossing, 0, slots // 2 * STEPS)
    singles = jnp.where(crossing, slots, 0)
    barrier = pltpu.get_barrier_semaphore()
    far_first = sorted(range(1, sectors), key=lambda k: abs(2 * k - sectors))
    for k in far_first:
        pl.semaphore_signal(
            barrier, 1, device_id={"sector": lax.rem(mine + k, sectors)}, device_id_type=MESH
        )
    for k in range(1, regions):
        pl.semaphore_signal(
            barrier, 1, device_id={"region": lax.rem(me + k, regions)}, device_id_type=MESH
        )
    small = [
        pltpu.make_async_copy(src, dst, small_sem.at[i])
        for i, (src, dst) in enumerate((
            (operator, operator_in), (live, live_in), (decay, decay_all.at[me]), (energy, energy_all.at[me]),
        ))
    ]
    for copy in small:
        copy.start()
    for n in range(slots):
        pltpu.make_async_copy(right.at[n], right_in.at[n], right_sem.at[n]).start()
        pltpu.make_async_copy(start.at[n], start_in.at[n], start_sem.at[n]).start()
    pl.semaphore_wait(barrier, regions + sectors - 2)

    def left_copy(n):
        return pltpu.make_async_remote_copy(
            src_ref=left.at[n], dst_ref=left_in.at[n],
            send_sem=left_send.at[n], recv_sem=left_recv.at[n],
            device_id={"region": lax.rem(me + 1, regions)}, device_id_type=MESH,
        )

    def own_copy(n):
        return pltpu.make_async_copy(left.at[n], left_in.at[n], left_recv.at[n])

    def prefix_copies(k, slot):
        to = {"region": lax.rem(me + k, regions)}
        return [
            pltpu.make_async_remote_copy(
                src_ref=src, dst_ref=dst.at[slot],
                send_sem=pre_send.at[i, k - 1], recv_sem=pre_recv.at[i, k - 1],
                device_id=to, device_id_type=MESH,
            )
            for i, (src, dst) in enumerate(((decay, decay_all), (energy, energy_all)))
        ]

    for k in range(1, regions):

        @pl.when(me + k < regions)
        def _():
            for copy in prefix_copies(k, me):
                copy.start()

    @pl.when(me < regions - 1)
    def _():
        for n in range(slots):
            left_copy(n).start()

    @pl.when(me == 0)
    def _():
        for n in range(slots):
            own_copy(n).start()

    for copy in small:
        copy.wait()
    live_slots = live_in[...]
    part[...] = jnp.zeros_like(part)

    lines[...] = operator_in[...].astype(F32)

    def where_one(test):
        return jnp.where(test, 1.0, 0.0).astype(BF16)

    def grid_of(shape):
        return [lax.broadcasted_iota(jnp.int32, shape, i) for i in range(2)]

    def spread_operator(out, swap):
        r, c = grid_of((side, chan * phys))
        u = (r // group) % chan
        if swap:
            u = u + 1 - 2 * (u % 2)
        pick_row = where_one((c // phys == u) & (c % phys == r // (chan * group)))
        r, c = grid_of((chan, side))
        total = jnp.zeros((side, side), F32)
        for t in range(phys):
            tall = jnp.dot(
                pick_row,
                lines[pl.ds(t, chan * phys, stride=phys), :].astype(BF16),
                preferred_element_type=F32,
            ).astype(BF16)
            pick_column = where_one((c // TILE == r) & (c % phys == t))
            total = total + jnp.dot(tall, pick_column, preferred_element_type=F32)
        r, c = grid_of((side, side))
        out[...] = jnp.where(r % group == (c // phys) % group, total, 0.0).astype(BF16)

    spread_operator(spread, False)
    spread_operator(flipped, True)

    def sum8(value):
        return jnp.sum(value.reshape(-1, 8, value.shape[-1]), axis=0)

    def spread_sum(total):
        return jnp.broadcast_to(jnp.sum(total, keepdims=True).reshape(1, 1), (1, blk))

    def length_of(square, whole):
        square = jnp.maximum(square, 1e-10 * whole)
        inverse = jnp.where(square > 0, lax.rsqrt(jnp.where(square > 0, square, 1.0)), 0.0)
        return square * inverse, inverse

    def share_of(value, norm):
        return jnp.where(norm > 0, value / jnp.where(norm > 0, norm, 1.0), 0.0)

    zero = jnp.zeros((8, blk), F32)
    lane = lax.broadcasted_iota(jnp.int32, (1, blk), 1)
    lane8 = lax.broadcasted_iota(jnp.int32, (8, blk), 1)
    line8 = lax.broadcasted_iota(jnp.int32, (8, blk), 0)
    chunk = 64

    def open_slot(n):
        pltpu.make_async_copy(right.at[n], right_in.at[n], right_sem.at[n]).wait()
        pltpu.make_async_copy(start.at[n], start_in.at[n], start_sem.at[n]).wait()
        alive = jnp.broadcast_to(jnp.where(n < live_slots, 1.0, 0.0), (1, blk)).astype(F32)
        total = zero
        for r in range(0, wide, chunk):
            first = start_in[n, r : r + chunk].astype(F32) * alive
            basis[n, 0, r : r + chunk] = first
            vector_a[n, r : r + chunk] = first.astype(BF16)
            vector_b[n, r : r + chunk] = first.astype(BF16)
            total = total + sum8(first * first)
            for i in range(1, STEPS):
                basis[n, i, r : r + chunk] = jnp.zeros((chunk, blk), F32)
        total = spread_sum(total)
        norms[n] = jnp.where(line8 == 0, total, 0.0)
        part[...] = jnp.where((line8 == n) & (lane8 == 8 * STEPS), total, part[...])

    low_rows = lax.broadcasted_iota(jnp.int32, (side, 2 * blk), 0) % (2 * group) < group

    def contract(n, vector, inner, mixed):
        half = wide // 2

        def right_part(h, w):
            side_by_side = jnp.concatenate([right_in[n, w], right_in[n, w + 1]], axis=1)
            inner[h * half : (h + 1) * half, w * blk : (w + 2) * blk] = jnp.dot(
                vector[n, h * half : (h + 1) * half], side_by_side, preferred_element_type=F32
            ).astype(BF16)

        def operator_part(q):
            def stacked(g):
                row = (4 * q + g) * TILE
                return jnp.concatenate(
                    [inner[row : row + TILE, w * blk : (w + 1) * blk] for w in range(chan)], axis=0
                )

            even = jnp.dot(
                spread[...], jnp.concatenate([stacked(0), stacked(2)], axis=1),
                preferred_element_type=F32,
            )
            odd = jnp.dot(
                flipped[...], jnp.concatenate([stacked(1), stacked(3)], axis=1),
                preferred_element_type=F32,
            )
            low = jnp.where(low_rows, even, odd)
            high = jnp.where(low_rows, odd, even)
            for s in range(phys):
                for m in range(chan // 2):
                    row = s * chan * group + m * 2 * group
                    for k, tile in enumerate((low, high)):
                        tile = tile[row : row + 2 * group]
                        if k:
                            tile = pltpu.roll(tile, group, 0)
                        tile = jnp.concatenate([tile[:, :blk], tile[:, blk:]], axis=0).astype(BF16)
                        at = (2 * m + k) * blk + q * TILE
                        mixed[at : at + TILE, s * blk : (s + 1) * blk] = tile

        rights = [functools.partial(right_part, h, w) for h in range(2) for w in range(0, chan, 2)]
        return rights, [functools.partial(operator_part, q) for q in range(wide // (4 * TILE))]

    def close(n, j, vector, mixed, value, final=False):
        known = j + 1 if isinstance(j, int) else STEPS
        held = {"along": [zero] * known, "whole": zero, "norm": zero}

        def left_part():
            rows = jnp.concatenate([left_in[n, u] for u in range(chan)], axis=1)
            result = jnp.dot(rows, mixed[...], preferred_element_type=F32)
            for s in range(phys):
                value[0, pl.ds(s, blk, stride=phys), :] = result[:, s * blk : (s + 1) * blk]

        def image_part(r):
            image = value[0, r : r + chunk] + column[n, r : r + chunk] * vector[n, r : r + chunk].astype(F32)
            value[0, r : r + chunk] = image
            held["whole"] = held["whole"] + sum8(image * image)
            held["along"] = [
                a + sum8(basis[n, i, r : r + chunk] * image) for i, a in enumerate(held["along"])
            ]

        def number_part():
            along, whole = [spread_sum(a) for a in held["along"]], spread_sum(held["whole"])
            shares = [share_of(a, norms[n, i : i + 1]) for i, a in enumerate(along)]
            square = whole
            for a, c in zip(along, shares):
                square = square - a * c
            held["shares"] = shares
            held["length"], held["inverse"] = length_of(square, whole)

        def probe_part(r):
            probe = value[here_zero, r : r + chunk]
            for i, c in enumerate(held["shares"]):
                probe = probe - c * basis[n + here_zero, i, r : r + chunk]
            probe = probe * held["inverse"]
            vector[n, r : r + chunk] = probe.astype(BF16)
            basis[n, j + 1, r : r + chunk] = probe
            held["norm"] = held["norm"] + sum8(probe * probe)

        def record_part():
            numbers = list(enumerate(held["shares"]))
            if not final:
                norm = spread_sum(held["norm"])
                norms[n] = jnp.where(line8 == j + 1, norm, norms[n])
                numbers += [(STEPS, held["length"]), (STEPS + 1, norm)]
            row = jnp.zeros((1, blk), F32)
            for i, number in numbers:
                row = jnp.where(lane == 8 * j + i, number, row)
            part[...] = jnp.where((line8 == n) & (lane8 // 8 == j), row, part[...])

        images = [functools.partial(image_part, r) for r in range(0, wide, chunk)]
        probes = [] if final else [functools.partial(probe_part, r) for r in range(0, wide, chunk)]
        return left_part, images, number_part, probes, record_part

    def run(parts):
        for one in parts:
            one()

    def beside(closing, contracting):
        left_part, images, number_part, probes, record_part = closing
        rights, operators = contracting
        run(rights[:4])
        left_part()
        run(rights[4:8])
        for k, one in enumerate(images):
            one()
            run(rights[8 + k : 9 + k])
        number_part()
        operators[0]()
        operators[1]()
        if not probes:
            record_part()
        for k, one in enumerate(probes):
            one()
            if k % 2:
                run(operators[2 + k // 2 : 3 + k // 2])
        run(operators[6 if probes else 2 :])
        if probes:
            record_part()

    def before(closing, contracting):
        left_part, images, number_part, probes, record_part = closing
        rights, operators = contracting
        left_part()
        run(images)
        number_part()
        run(probes[:4])
        for k, one in enumerate(probes[4:]):
            run(rights[2 * k : 2 * k + 2])
            one()
        run(rights[8:])
        record_part()
        run(operators)

    def alone(closing):
        left_part, images, number_part, probes, record_part = closing
        left_part()
        run(images)
        number_part()
        run(probes)
        record_part()

    for n in range(slots):
        open_slot(n)
    for parts in contract(0, vector_a, inner_a, mixed_a):
        run(parts)

    for k in range(1, regions):

        @pl.when(me + k < regions)
        def _():
            for copy in prefix_copies(k, me):
                copy.wait_send()

        @pl.when(me >= k)
        def _():
            for copy in prefix_copies(k, lax.rem(me + regions - k, regions)):
                copy.wait_recv()

    offsets = jnp.zeros((slots, blk), F32)
    for p in range(regions - 1):
        offsets = jnp.where(p < me, decay_all[p] * offsets + energy_all[p], offsets)
    for n in range(slots):
        turned = jnp.broadcast_to(offsets[n : n + 1], (blk, blk)).T
        for s in range(phys):
            column[n, pl.ds(s, blk, stride=phys), :] = turned

    @pl.when(jnp.logical_not(crossing))
    def _():
        for n in range(slots):
            own_copy(n).wait()

    def both(i, carry):
        n, j = i // STEPS * 2, i % STEPS
        after = (i + 1) % (slots // 2 * STEPS)
        beside(close(n, j, vector_a, mixed_a, value_a), contract(n + 1, vector_b, inner_b, mixed_b))
        beside(
            close(n + 1, j, vector_b, mixed_b, value_b),
            contract(after // STEPS * 2, vector_a, inner_a, mixed_a),
        )
        return carry

    lax.fori_loop(0, rounds, both, 0)

    def single(n, carry):
        own_copy(n).wait()
        chain = vector_b, inner_b, mixed_b
        before(close(n, 0, vector_b, mixed_a, value_b), contract(n, *chain))
        before(close(n, 1, vector_b, mixed_b, value_b), contract(n, *chain))

        def last():
            return close(n, STEPS - 1, vector_b, mixed_b, value_b, final=True)

        @pl.when(n < slots - 1)
        def _():
            beside(last(), contract(n + 1, vector_a, inner_a, mixed_a))

        @pl.when(n == slots - 1)
        def _():
            alone(last())

        return carry

    lax.fori_loop(0, singles, single, 0)

    gathered[mine] = part[...]

    def copy_of(k, slot):
        return pltpu.make_async_remote_copy(
            src_ref=part, dst_ref=gathered.at[slot],
            send_sem=sum_send.at[k - 1], recv_sem=sum_recv.at[k - 1],
            device_id={"sector": lax.rem(mine + k, sectors)}, device_id_type=MESH,
        )

    for k in far_first:
        copy_of(k, mine).start()
    for k in range(1, sectors):
        copy_of(k, lax.rem(mine + sectors - k, sectors)).wait()
    many = sectors * 8
    table = gathered[...].reshape(many, blk).T
    images = [[table[8 * j + i : 8 * j + i + 1] for i in range(STEPS)] + [None] for j in range(STEPS)]
    gram = {0: table[8 * STEPS : 8 * STEPS + 1]}
    for j in range(STEPS):
        length = table[8 * j + STEPS : 8 * j + STEPS + 1]
        images[j] = [c if i <= j else None for i, c in enumerate(images[j])]
        images[j][j + 1] = length
        gram[j + 1] = table[8 * j + STEPS + 1 : 8 * j + STEPS + 2]

    def inner(x, y):
        total = jnp.zeros((1, many), F32)
        for i, (xi, yi) in enumerate(zip(x, y)):
            if xi is not None and yi is not None:
                total = total + xi * yi * gram[i]
        return jnp.broadcast_to(jnp.sum(total, axis=1, keepdims=True), (1, many))

    def mix(p, x, q, y):
        def one(a, b):
            if a is None:
                return None if b is None else q * b
            return p * a if b is None else p * a + q * b

        return [one(a, b) for a, b in zip(x, y)]

    unit = jnp.ones((1, many), F32)
    inverse = lax.rsqrt(inner([unit] + [None] * STEPS, [unit] + [None] * STEPS) + EPS)
    current = [inverse * unit, None, None, None]
    applied = [inverse * a if a is not None else None for a in images[0]]
    for _ in range(DAV):
        quotient = inner(current, applied)
        residual = mix(1.0, applied, -quotient, current)
        resid_sq = inner(residual, residual)
        factor = lax.rsqrt(resid_sq + EPS)
        search = [factor * a if a is not None else None for a in residual]
        moved = [None] * (STEPS + 1)
        for a, line in zip(search, images):
            if a is not None:
                moved = mix(1.0, moved, a, line)
        curvature = inner(search, moved)
        cos_part, sin_part = half_rotation(-2.0 * resid_sq * factor, curvature - quotient)
        current = mix(cos_part, current, sin_part, search)
        applied = mix(cos_part, applied, sin_part, moved)
    energy_buf[...] = jnp.broadcast_to(inner(current, applied)[:, :1], (8, blk))
    scale = math.sqrt(slots * sectors * blk * phys * blk)

    copies = [pltpu.make_async_copy(energy_buf, energy_out, out_sem.at[slots])]
    copies[0].start()
    for n in range(slots):
        here = lax.broadcasted_iota(jnp.int32, (1, many), 1) == mine * 8 + n
        factors = [
            jnp.broadcast_to(jnp.sum(jnp.where(here, scale * c, 0.0), axis=1, keepdims=True), (1, blk))
            for c in current[:STEPS]
        ]
        for r in range(0, wide, chunk):
            state = jnp.zeros((chunk, blk), F32)
            for i, c in enumerate(factors):
                state = state + c * basis[n, i, r : r + chunk]
            state_buf[n, r : r + chunk] = state.astype(BF16)
        copies.append(pltpu.make_async_copy(state_buf.at[n], state_out.at[n], out_sem.at[n]))
        copies[-1].start()
    for copy in copies:
        copy.wait()

    @pl.when(me < regions - 1)
    def _():
        for n in range(slots):
            left_copy(n).wait_send()


def finish(state, energy, out, density, energy_out, rows_buf, density_buf, energy_buf, sems):
    slots, wide, blk = state.shape
    phys = wide // blk
    energy_buf[0] = energy[0, 0]
    copies = [
        pltpu.make_async_copy(state, out, sems.at[slots]),
        pltpu.make_async_copy(energy_buf, energy_out, sems.at[slots + 1]),
    ]
    for copy in copies:
        copy.start()
    for n in range(slots):
        rows_buf[n] = state[n].astype(F32)
        total = jnp.zeros((blk, blk), F32)
        for s in range(phys):
            rows = rows_buf[n, pl.ds(s, blk, stride=phys), :].astype(BF16)
            total = total + lax.dot_general(
                rows, rows, (((1,), (1,)), ((), ())), preferred_element_type=F32
            )
        density_buf[n] = total / (phys * blk)
        copies.append(pltpu.make_async_copy(density_buf.at[n], density.at[n], sems.at[n]))
        copies[-1].start()
    for copy in copies:
        copy.wait()


def body(regions, sectors, start_state, left_env, right_env, mpo_tensor, decay, energy_terms, live_count):
    _, slots, blk, phys, _ = start_state.shape
    chan = left_env.shape[2]
    wide = phys * blk
    side = chan * TILE
    vmem = pl.BlockSpec(memory_space=pltpu.VMEM)
    hbm = pl.BlockSpec(memory_space=pltpu.HBM)
    dma = pltpu.SemaphoreType.DMA
    twice = lambda *spec: [pltpu.VMEM(*spec)] * 2
    outs = pl.pallas_call(
        functools.partial(kernel, regions, sectors),
        out_shape=(
            jax.ShapeDtypeStruct((slots, wide, blk), BF16),
            jax.ShapeDtypeStruct((8, blk), F32),
        ),
        in_specs=[hbm] * 7,
        out_specs=(hbm, hbm),
        scratch_shapes=[
            pltpu.VMEM((chan * phys * phys, chan), BF16),
            pltpu.VMEM((1, 1), jnp.int32),
            pltpu.VMEM((slots, wide, blk), BF16),
            pltpu.VMEM((8, blk), F32),
            pltpu.VMEM((slots, wide, blk), BF16),
            pltpu.VMEM((slots, chan, blk, blk), BF16),
            pltpu.VMEM((slots, chan, blk, blk), BF16),
            pltpu.VMEM((chan * phys * phys, chan), F32),
            *twice((side, side), BF16),
            pltpu.VMEM((slots, wide, blk), F32),
            *twice((slots, wide, blk), BF16),
            *twice((wide, chan * blk), BF16),
            *twice((chan * blk, wide), BF16),
            *twice((1, wide, blk), F32),
            pltpu.VMEM((slots, STEPS + 1, wide, blk), F32),
            pltpu.VMEM((slots, 8, blk), F32),
            pltpu.VMEM((regions, slots, blk), F32),
            pltpu.VMEM((regions, slots, blk), F32),
            pltpu.VMEM((8, blk), F32),
            pltpu.VMEM((sectors, 8, blk), F32),
            dma((slots,)), dma((slots,)), dma((slots,)), dma((slots,)), dma((4,)), dma((slots + 1,)),
            dma((2, regions)), dma((2, regions)),
            dma((sectors,)), dma((sectors,)),
        ],
        compiler_params=pltpu.CompilerParams(
            collective_id=0, has_side_effects=True, vmem_limit_bytes=60 * 2**20
        ),
    )(
        start_state.reshape(slots, wide, blk), left_env[0], right_env[0],
        mpo_tensor.reshape(chan * phys * phys, chan),
        decay[0], energy_terms[0], live_count,
    )
    state_out, density, energy = pl.pallas_call(
        finish,
        out_shape=(
            jax.ShapeDtypeStruct((slots, wide, blk), BF16),
            jax.ShapeDtypeStruct((slots, blk, blk), F32),
            jax.ShapeDtypeStruct((1,), F32),
        ),
        in_specs=[vmem, vmem],
        out_specs=(hbm, hbm, hbm),
        scratch_shapes=[
            pltpu.VMEM((slots, wide, blk), F32),
            pltpu.VMEM((slots, blk, blk), F32),
            pltpu.SMEM((1,), F32),
            dma((slots + 2,)),
        ],
    )(*outs)
    return (
        state_out.reshape(start_state.shape),
        density.reshape(1, slots, blk, blk),
        energy,
    )


def solution(mesh):
    in_specs = (
        P("region", "sector", None, None, None),
        P("region", "sector", None, None, None),
        P("region", "sector", None, None, None),
        P(),
        P("region", "sector", None),
        P("region", "sector", None),
        P("region", "sector"),
    )
    out_specs = (
        P("region", "sector", None, None, None),
        P("region", "sector", None, None),
        P("region"),
    )
    step = functools.partial(body, mesh.shape["region"], mesh.shape["sector"])
    return jax.shard_map(step, mesh=mesh, in_specs=in_specs, out_specs=out_specs, check_vma=False)
```
